32 devices in a mesh: row: 8 (over z, core), col: 4 (over y, x).
Axes of the slice: x: 2, y: 2, z: 4, core: 2. Of those that a mesh axis runs over, the one named last changes fastest.
Arguments:
- pair_elems: bfloat16 [320, 12288], P('row', 'col'), may hold values from -0.59765625 to 0.59765625
- counts: int32 [8], replicated, may hold values from 1 to 40, 200 in all
- val_band: int32 [320], replicated, may hold values from 0 to 127
- cond_band: int32 [320], replicated, may hold values from 0 to 511
- val_energy: float32 [128], replicated, may hold values from -12 to -0.5
- cond_energy: float32 [512], replicated, may hold values from 0.5 to 12
- frequency: float32 [3], replicated, may hold values from 0.3 to 6
Outputs:
- chi: float32 [3, 12288, 12288], P(None, 'row', 'col')
The draws below stay inside these ranges and needn't reach their ends.
Inputs may be any that keep to these rules, and one draw needn't show every extreme that they name: counts sum to 200, and the largest is 40.
All inputs are finite; a program needn't handle non-finite values.
Results may differ from the reference program's by a relative error of at most 0.0028.
Values may be sent and summed in bfloat16 or wider, within the bound.
A program may use at most 128 MiB of HBM per device.

```python
import math
import jax
import jax.numpy as jnp
import numpy as np
from jax import lax

NPW = 12288
NVAL = 128
NCOND = 512
NFREQ = 3
CAP = 40
SLOTS = 320
TOTAL = 200
N_ROW = 8


def touch_ends(result, rng, smallest, largest):
    place = [jax.random.randint(jax.random.fold_in(rng, axis), (), 0, length) for axis, length in enumerate(result.shape)]
    widest = result.shape.index(max(result.shape))
    neighbour = place[:widest] + [(place[widest] + 1) % result.shape[widest]] + place[widest + 1:]
    return result.at[tuple(place)].set(smallest).at[tuple(neighbour)].set(largest)


def levels(rng, extent, cuts, least, top_value):
    loudness = 1.0
    for dim, shards_of in cuts:
        heights = jax.random.uniform(jax.random.fold_in(jax.random.fold_in(rng, 6), dim), (shards_of,), jnp.float32, least / len(cuts), top_value / len(cuts))
        loudness = loudness * jnp.repeat(jnp.exp(heights), extent[dim] // shards_of).reshape((-1,) + (1,) * (len(extent) - 1 - dim))
    return loudness


def profile(count, total, bound, slope):
    portions = [(1 << 20) // math.isqrt(rank ** slope) + 1 for rank in range(2, count + 1)]
    rest, holding = total - bound - (count - 1), [1] * (count - 1)
    while rest > 0:
        movable = [i for i in range(count - 1) if holding[i] < bound]
        mass, left = sum([portions[i] for i in movable]), rest
        for i in movable:
            more = min(bound - holding[i], max(1, left * portions[i] // mass), rest)
            holding[i] = holding[i] + more
            rest = rest - more
    return np.array([bound] + holding)


def ragged(rng, amount, total, reach, slope):
    if amount == 2:
        one = jax.random.randint(rng, (), max(1, total - reach), min(reach, total - 1) + 1)
        return jnp.stack([one, total - one])
    lengths = jnp.asarray(profile(amount, total, reach, slope), jnp.int32)
    pairs = (amount - 1) // 2
    donor, sink = lengths[1:1 + 2 * pairs:2], lengths[2:2 + 2 * pairs:2]
    margin = jnp.minimum(donor - 1, reach - sink)
    moved = jax.random.randint(jax.random.fold_in(rng, 1), (pairs,), 0, 1 << 20) % (margin + 1)
    lengths = lengths.at[1:1 + 2 * pairs:2].set(donor - moved).at[2:2 + 2 * pairs:2].set(sink + moved)
    return lengths[jax.random.permutation(jax.random.fold_in(rng, 2), amount)]


def normal_values(key, extent, spread, limit, shards=(), kind=jnp.bfloat16):
    entries = jax.random.normal(key, extent, jnp.float32) * spread
    if len(shards) > 0:
        entries = levels(key, extent, shards, -0.22, 0.18) * entries
    return jnp.clip(entries, min=-limit, max=limit).astype(kind)


def setup_inputs(seed: int = 0) -> dict:
    seeds = jax.random.split(jax.random.key(seed), 8)
    pair_elems = normal_values(seeds[0], (SLOTS, NPW), 0.1, 0.59765625, ((0, 8), (1, 4)))
    counts = ragged(seeds[1], N_ROW, TOTAL, CAP, 2).astype(jnp.int32)
    val_band = touch_ends(jax.random.randint(seeds[2], (SLOTS,), 0, NVAL), jax.random.fold_in(seeds[2], 1), 0, NVAL - 1).astype(jnp.int32)
    cond_band = touch_ends(jax.random.randint(seeds[3], (SLOTS,), 0, NCOND), jax.random.fold_in(seeds[3], 1), 0, NCOND - 1).astype(jnp.int32)
    val_energy = jnp.clip(jax.random.uniform(seeds[4], (NVAL,), jnp.float32, -12.0, -0.5), -12.0, -0.5)
    cond_energy = jnp.clip(jax.random.uniform(seeds[5], (NCOND,), jnp.float32, 0.5, 12.0), 0.5, 12.0)
    frequency = jnp.clip(jnp.exp(jax.random.uniform(seeds[6], (NFREQ,), jnp.float32, math.log(0.3), math.log(6.0))), 0.3, 6.0)
    return dict(pair_elems=pair_elems, counts=counts, val_band=val_band, cond_band=cond_band, val_energy=val_energy, cond_energy=cond_energy, frequency=frequency)


def reference(pair_elems, counts, val_band, cond_band, val_energy, cond_energy, frequency):
    live_mask = (jnp.arange(CAP, dtype=jnp.int32)[None, :] < counts[:, None]).astype(jnp.float32).reshape(-1)
    energy_gap = jnp.take(cond_energy, cond_band) - jnp.take(val_energy, val_band)
    weights = -4.0 * live_mask[None, :] * energy_gap[None, :] / (energy_gap[None, :] ** 2 + frequency[:, None] ** 2)
    elements = pair_elems.astype(jnp.float32)

    def one_frequency(weight_row):
        scaled = (elements * weight_row[:, None]).astype(jnp.bfloat16)
        return lax.dot_general(scaled, pair_elems, (((0,), (0,)), ((), ())), preferred_element_type=jnp.float32)

    return lax.map(one_frequency, weights)
```

```python
import functools
import math

import jax
import jax.numpy as jnp
from jax import lax
from jax.experimental import pallas as pl
from jax.experimental.pallas import tpu as pltpu
from jax.sharding import PartitionSpec as P

MESH = pl.DeviceIdType.MESH
LAG = 3
TILE = 1024
VMEM = 67043328
SPARE = 1024 * 1024


def ring_place(c, count):
    if count == 4:
        return c + (c // 2) * (1 - 2 * (c % 2))
    return c


def gather_kernel(rows, cols, halves, x_ref, counts_hbm, freq_hbm, val_band_hbm, cond_band_hbm, val_energy_hbm,
                  cond_energy_hbm, cols_ref, seg_ref, choose_ref, weights_ref, counts_ref, freq_ref, val_band, cond_band,
                  val_energy, cond_energy, small_sem, own_sem, line_send, line_recv, mate_send, mate_recv, enter_send,
                  relay_send, ring_recv):
    r, c = lax.axis_index("row"), lax.axis_index("col")
    chips = rows // 2
    q, k = r // 2, r % 2
    pieces, lane = cols_ref.shape[1], cols_ref.shape[3]
    ratio = rows // cols
    chunks = ratio * halves
    place = ring_place(c, cols)
    source = r // ratio
    ring_next = [ring_place((place + 1) % cols, cols), ring_place((place + cols - 1) % cols, cols)]
    ahead = (place - ring_place(source, cols) + cols) % cols
    hops = [ahead, cols - ahead]
    up_ok, down_ok = q + 1 < chips, q >= 1

    own = [
        pltpu.make_async_copy(x_ref.at[:, pl.ds(p * lane, lane)], cols_ref.at[r, p], own_sem.at[p])
        for p in range(pieces)
    ]
    small = [
        pltpu.make_async_copy(src, dst, small_sem.at[i])
        for i, (src, dst) in enumerate((
            (counts_hbm, counts_ref), (freq_hbm, freq_ref), (val_band_hbm, val_band), (cond_band_hbm, cond_band),
            (val_energy_hbm, val_energy), (cond_energy_hbm, cond_energy),
        ))
    ]
    for copy in own + small:
        copy.start()
    barrier = pltpu.get_barrier_semaphore()

    def greet(row, col):
        pl.semaphore_signal(barrier, inc=1, device_id=(row, col), device_id_type=MESH)

    mate = 2 * q + 1 - k
    greet(mate, c)
    for nxt in ring_next:
        greet(2 * q, nxt)
        greet(2 * q + 1, nxt)

    @pl.when(up_ok)
    def _():
        greet(r + 2, c)

    @pl.when(down_ok)
    def _():
        greet(r - 2, c)

    pl.semaphore_wait(barrier, 5 + up_ok.astype(jnp.int32) + down_ok.astype(jnp.int32))
    for copy in own:
        copy.wait()

    def remote(src, dst, send, recv, row, col):
        return pltpu.make_async_remote_copy(
            src_ref=src, dst_ref=dst, send_sem=send, recv_sem=recv, device_id=(row, col), device_id_type=MESH
        )

    def block_of(stream, d, core):
        return 2 * (q - d if stream == 0 else q + d) + core

    def has(stream, d):
        return q >= d if stream == 0 else q + d < chips

    def line_copy(stream, d, j, b):
        ref = cols_ref.at[b, pl.ds(2 * j, 2)]
        row = r + 2 if stream == 0 else r - 2
        return remote(ref, ref, line_send.at[stream, d, j], line_recv.at[stream, d, j], row, c)

    def line_arrival(stream, d, j, b):
        ref = cols_ref.at[b, pl.ds(2 * j, 2)]
        return remote(ref, ref, line_send.at[stream, d, j], line_recv.at[stream, d - 1, j], mate, c)

    def mate_copy(b, j):
        ref = cols_ref.at[b, pl.ds(2 * j, 2)]
        return remote(ref, ref, mate_send.at[b, j], mate_recv.at[b, j], mate, c)

    def enter_copy(b, j, way):
        g = c * ratio + j // halves
        src = cols_ref.at[b, 2 * j + way]
        dst = seg_ref.at[b, 2 * (j % halves) + way]
        return remote(src, dst, enter_send.at[b, j, way], ring_recv.at[b, j % halves, way], g, ring_next[way])

    def relay_copy(b, j, way):
        ref = seg_ref.at[b, 2 * (j % halves) + way]
        return remote(ref, ref, relay_send.at[b, j % halves, way], ring_recv.at[b, j % halves, way], r, ring_next[way])

    def feeds(j):
        return (c * ratio + j // halves) // 2 == q

    def relays(j):
        return (source != c) & (j // halves == r % ratio)

    def onward(stream):
        return up_ok if stream == 0 else down_ok

    def line_part(step):
        d, j = step // chunks, step % chunks
        for stream in (0, 1):
            here = has(stream, d) if stream == 0 else has(stream, d) & (d > 0)
            b = block_of(stream, d, k)

            @pl.when(has(stream, d))
            def _():
                @pl.when(d > 0)
                def _():
                    line_arrival(stream, d, j, b).wait_recv()

                @pl.when(onward(stream))
                def _():
                    line_copy(stream, d, j, b).start()

            @pl.when(here)
            def _():
                mate_copy(b, j).start()

                @pl.when(feeds(j))
                def _():
                    for way in (0, 1):
                        enter_copy(b, j, way).start()

    def ring_part(step, way):
        d, j = step // chunks, step % chunks

        @pl.when(relays(j))
        def _():
            for stream in (0, 1):
                here = has(stream, d) if stream == 0 else has(stream, d) & (d > 0)

                @pl.when(here)
                def _():
                    for core in (0, 1):
                        b = block_of(stream, d, core)
                        relay_copy(b, j, way).wait_recv()

                        @pl.when(ring_next[way] != source)
                        def _():
                            relay_copy(b, j, way).start()

    steps = chunks * chips

    def body(step, carry):
        @pl.when(step < steps)
        def _():
            line_part(step)

        for way in (0, 1):
            late = step - LAG * hops[way]

            @pl.when((late >= 0) & (late < steps))
            def _():
                ring_part(late, way)

        return carry

    lax.fori_loop(0, chunks, body, 0)
    for copy in small:
        copy.wait()
    capacity, (depth, slots) = x_ref.shape[0], choose_ref.shape
    place_of = slot_target(counts_ref, (1, slots), 1, capacity)
    choose = (lax.broadcasted_iota(jnp.int32, (depth, slots), 0) == place_of).astype(jnp.float32)
    gap = pick(cond_band, cond_energy) - pick(val_band, val_energy)
    gap = lax.dot_general(
        gap, choose, (((1,), (1,)), ((), ())), precision=lax.Precision.HIGHEST, preferred_element_type=jnp.float32
    )
    for f in range(weights_ref.shape[0]):
        weights_ref[f] = -4.0 * gap / (gap * gap + freq_ref[f] * freq_ref[f])
    choose_ref[...] = choose.astype(jnp.bfloat16)
    lax.fori_loop(chunks, steps + LAG * (cols - 1), body, 0)

    def finish(step, carry):
        d, j = step // chunks, step % chunks
        for stream in (0, 1):
            here = has(stream, d) if stream == 0 else has(stream, d) & (d > 0)
            b = block_of(stream, d, k)
            theirs = block_of(stream, d, 1 - k)

            @pl.when(has(stream, d) & onward(stream))
            def _():
                line_copy(stream, d, j, b).wait_send()

            @pl.when(here)
            def _():
                mate_copy(b, j).wait_send()
                mate_copy(theirs, j).wait_recv()

                @pl.when(feeds(j))
                def _():
                    for way in (0, 1):
                        enter_copy(b, j, way).wait_send()

                @pl.when(relays(j))
                def _():
                    for core in (0, 1):
                        e = block_of(stream, d, core)
                        for way in (0, 1):
                            @pl.when(ring_next[way] != source)
                            def _():
                                relay_copy(e, j, way).wait_send()

        return carry

    lax.fori_loop(0, steps, finish, 0)

    @pl.when(source == c)
    def _():
        here = pltpu.make_async_copy(cols_ref.at[:, pl.ds((r % ratio) * 2 * halves, 2 * halves)], seg_ref, own_sem.at[0])
        here.start()
        here.wait()


def gather(x, counts, frequency, val_band, cond_band, val_energy, cond_energy, rows, cols):
    capacity, width = x.shape
    slots = rows * capacity
    live = slots * 5 // 8
    depth = pl.cdiv(live, 256) * 256
    ratio = rows // cols
    seg_width = width // ratio
    halves = 2 if seg_width % 512 == 0 else 1
    chunks, chips = ratio * halves, rows // 2
    dma = pltpu.SemaphoreType.DMA
    room = 2 * (slots * (width + seg_width) + depth * slots) + 4 * 8 * depth * frequency.shape[0]
    return pl.pallas_call(
        functools.partial(gather_kernel, rows, cols, halves),
        out_shape=(
            pltpu.VMEM((rows, 2 * chunks, capacity, seg_width // halves // 2), x.dtype),
            pltpu.VMEM((rows, 2 * halves, capacity, seg_width // halves // 2), x.dtype),
            pltpu.VMEM((depth, slots), jnp.bfloat16),
            pltpu.VMEM((frequency.shape[0], 8, depth), jnp.float32),
        ),
        in_specs=[pl.BlockSpec(memory_space=pl.ANY)] * 7,
        out_specs=[pl.BlockSpec(memory_space=pltpu.VMEM)] * 4,
        scratch_shapes=[
            pltpu.SMEM(counts.shape, counts.dtype),
            pltpu.SMEM(frequency.shape, frequency.dtype),
            pltpu.VMEM(val_band.shape, val_band.dtype),
            pltpu.VMEM(cond_band.shape, cond_band.dtype),
            pltpu.VMEM(val_energy.shape, val_energy.dtype),
            pltpu.VMEM(cond_energy.shape, cond_energy.dtype),
            dma((6,)),
            dma((2 * chunks,)),
            dma((2, chips, chunks)),
            dma((2, chips, chunks)),
            dma((rows, chunks)),
            dma((rows, chunks)),
            dma((rows, chunks, 2)),
            dma((rows, halves, 2)),
            dma((rows, halves, 2)),
        ],
        compiler_params=pltpu.CompilerParams(
            collective_id=0, has_side_effects=True, vmem_limit_bytes=VMEM - room - SPARE
        ),
    )(x, counts, frequency, val_band, cond_band, val_energy, cond_energy)


def exact_dot(a, b):
    return lax.dot_general(
        a, b, (((1,), (0,)), ((), ())), precision=lax.Precision.HIGHEST, preferred_element_type=jnp.float32
    )


def pick(band_ref, table_ref):
    levels, slots = table_ref.shape[0], band_ref.shape[0]
    hit = lax.broadcasted_iota(jnp.int32, (levels, slots), 0) == band_ref[...][None, :]
    return exact_dot(jnp.broadcast_to(table_ref[...][None, :], (8, levels)), hit.astype(jnp.float32))


def slot_target(counts_ref, shape, axis, capacity):
    slot = lax.broadcasted_iota(jnp.int32, shape, axis)
    target = jnp.full(shape, -1, jnp.int32)
    before = 0
    for block in range(counts_ref.shape[0]):
        inside = slot - block * capacity
        live = (inside >= 0) & (inside < counts_ref[block])
        target = jnp.where(live, inside + before, target)
        before = before + counts_ref[block]
    return target


def product_kernel(weights, choose_ref, seg_ref, cols_ref, out_ref, packed, turned, scaled):
    which, n = pl.program_id(0), pl.program_id(1)
    tile = out_ref.shape[2]
    rows, pieces, capacity, lane = cols_ref.shape
    slots = rows * capacity

    @pl.when((n == 0) & (which == 0))
    def _():
        choose = choose_ref[...]
        for p in range(pieces):
            piece = cols_ref[:, p].reshape(slots, lane)
            packed[:, p * lane : (p + 1) * lane] = jnp.dot(
                choose, piece, preferred_element_type=jnp.float32
            ).astype(jnp.bfloat16)
        for p in range(seg_ref.shape[1]):
            piece = seg_ref[:, p].reshape(slots, lane)
            turned[p * lane : (p + 1) * lane, :] = lax.dot_general(
                piece, choose, (((0,), (1,)), ((), ())), preferred_element_type=jnp.float32
            ).astype(jnp.bfloat16)

    @pl.when(n == 0)
    def _():
        scaled[...] = (turned[...].astype(jnp.float32) * weights[which][:1]).astype(jnp.bfloat16)

    start = pl.multiple_of(n * tile, tile)
    out_ref[0] = jnp.dot(scaled[...], packed[:, pl.ds(start, tile)], preferred_element_type=jnp.float32)


def product(weights, choose, seg, columns):
    freqs = weights.shape[0]
    rows, pieces, capacity, lane = columns.shape
    width, seg_width = pieces * lane, seg.shape[1] * lane
    depth = choose.shape[0]
    tile = math.gcd(width, TILE)
    vmem = pl.BlockSpec(memory_space=pltpu.VMEM)
    return pl.pallas_call(
        product_kernel,
        out_shape=jax.ShapeDtypeStruct((freqs, seg_width, width), jnp.float32),
        grid=(freqs, width // tile),
        in_specs=[vmem] * 4,
        out_specs=pl.BlockSpec((1, seg_width, tile), lambda f, n: (f, 0, n)),
        scratch_shapes=[
            pltpu.VMEM((depth, width), jnp.bfloat16),
            pltpu.VMEM((seg_width, depth), jnp.bfloat16),
            pltpu.VMEM((seg_width, depth), jnp.bfloat16),
        ],
        compiler_params=pltpu.CompilerParams(vmem_limit_bytes=40 * 1024 * 1024),
    )(weights, choose, seg, columns)


def per_device(pair_elems, counts, val_band, cond_band, val_energy, cond_energy, frequency):
    rows, cols = lax.axis_size("row"), lax.axis_size("col")
    columns, seg, choose, weights = gather(
        pair_elems, counts, frequency, val_band, cond_band, val_energy, cond_energy, rows, cols
    )
    return product(weights, choose, seg, columns)


def solution(mesh):
    in_specs = (P("row", "col"), P(), P(), P(), P(), P(), P())
    out_specs = P(None, "row", "col")
    return jax.shard_map(
        per_device, mesh=mesh, in_specs=in_specs, out_specs=out_specs, check_vma=False
    )
```

```python
import functools
import math

import jax
import jax.numpy as jnp
from jax import lax
from jax.experimental import pallas as pl
from jax.experimental.pallas import tpu as pltpu
from jax.sharding import PartitionSpec as P

MESH = pl.DeviceIdType.MESH
LAG = 3
TILE = 1024
VMEM = 67043328
SPARE = 1024 * 1024
PIECES = 8
PARTS = 4
BUFFERS = 3
END_LAG = 3
MIDDLE_LAG = 4


def ring_place(c, count):
    if count == 4:
        return c + (c // 2) * (1 - 2 * (c % 2))
    return c


def gather_kernel(rows, cols, halves, x_ref, counts_hbm, freq_hbm, val_band_hbm, cond_band_hbm, val_energy_hbm,
                  cond_energy_hbm, cols_ref, seg_ref, choose_ref, weights_ref, counts_ref, freq_ref, val_band, cond_band,
                  val_energy, cond_energy, small_sem, own_sem, line_send, line_recv, mate_send, mate_recv, enter_send,
                  relay_send, ring_recv):
    r, c = lax.axis_index("row"), lax.axis_index("col")
    chips = rows // 2
    q, k = r // 2, r % 2
    pieces, lane = cols_ref.shape[1], cols_ref.shape[3]
    ratio = rows // cols
    chunks = ratio * halves
    place = ring_place(c, cols)
    source = r // ratio
    ring_next = [ring_place((place + 1) % cols, cols), ring_place((place + cols - 1) % cols, cols)]
    ahead = (place - ring_place(source, cols) + cols) % cols
    hops = [ahead, cols - ahead]
    up_ok, down_ok = q + 1 < chips, q >= 1

    own = [
        pltpu.make_async_copy(x_ref.at[:, pl.ds(p * lane, lane)], cols_ref.at[r, p], own_sem.at[p])
        for p in range(pieces)
    ]
    small = [
        pltpu.make_async_copy(src, dst, small_sem.at[i])
        for i, (src, dst) in enumerate((
            (counts_hbm, counts_ref), (freq_hbm, freq_ref), (val_band_hbm, val_band), (cond_band_hbm, cond_band),
            (val_energy_hbm, val_energy), (cond_energy_hbm, cond_energy),
        ))
    ]
    for copy in own + small:
        copy.start()
    barrier = pltpu.get_barrier_semaphore()

    def greet(row, col):
        pl.semaphore_signal(barrier, inc=1, device_id=(row, col), device_id_type=MESH)

    mate = 2 * q + 1 - k
    greet(mate, c)
    for nxt in ring_next:
        greet(2 * q, nxt)
        greet(2 * q + 1, nxt)

    @pl.when(up_ok)
    def _():
        greet(r + 2, c)

    @pl.when(down_ok)
    def _():
        greet(r - 2, c)

    pl.semaphore_wait(barrier, 5 + up_ok.astype(jnp.int32) + down_ok.astype(jnp.int32))
    for copy in own:
        copy.wait()

    def remote(src, dst, send, recv, row, col):
        return pltpu.make_async_remote_copy(
            src_ref=src, dst_ref=dst, send_sem=send, recv_sem=recv, device_id=(row, col), device_id_type=MESH
        )

    def block_of(stream, d, core):
        return 2 * (q - d if stream == 0 else q + d) + core

    def has(stream, d):
        return q >= d if stream == 0 else q + d < chips

    def line_copy(stream, d, j, b):
        ref = cols_ref.at[b, pl.ds(2 * j, 2)]
        row = r + 2 if stream == 0 else r - 2
        return remote(ref, ref, line_send.at[stream, d, j], line_recv.at[stream, d, j], row, c)

    def line_arrival(stream, d, j, b):
        ref = cols_ref.at[b, pl.ds(2 * j, 2)]
        return remote(ref, ref, line_send.at[stream, d, j], line_recv.at[stream, d - 1, j], mate, c)

    def mate_copy(b, j):
        ref = cols_ref.at[b, pl.ds(2 * j, 2)]
        return remote(ref, ref, mate_send.at[b, j], mate_recv.at[b, j], mate, c)

    def enter_copy(b, j, way):
        g = c * ratio + j // halves
        src = cols_ref.at[b, 2 * j + way]
        dst = seg_ref.at[b, 2 * (j % halves) + way]
        return remote(src, dst, enter_send.at[b, j, way], ring_recv.at[b, j % halves, way], g, ring_next[way])

    def relay_copy(b, j, way):
        ref = seg_ref.at[b, 2 * (j % halves) + way]
        return remote(ref, ref, relay_send.at[b, j % halves, way], ring_recv.at[b, j % halves, way], r, ring_next[way])

    def feeds(j):
        return (c * ratio + j // halves) // 2 == q

    def relays(j):
        return (source != c) & (j // halves == r % ratio)

    def onward(stream):
        return up_ok if stream == 0 else down_ok

    def line_part(step):
        d, j = step // chunks, step % chunks
        for stream in (0, 1):
            here = has(stream, d) if stream == 0 else has(stream, d) & (d > 0)
            b = block_of(stream, d, k)

            @pl.when(has(stream, d))
            def _():
                @pl.when(d > 0)
                def _():
                    line_arrival(stream, d, j, b).wait_recv()

                @pl.when(onward(stream))
                def _():
                    line_copy(stream, d, j, b).start()

            @pl.when(here)
            def _():
                mate_copy(b, j).start()

                @pl.when(feeds(j))
                def _():
                    for way in (0, 1):
                        enter_copy(b, j, way).start()

    def ring_part(step, way):
        d, j = step // chunks, step % chunks

        @pl.when(relays(j))
        def _():
            for stream in (0, 1):
                here = has(stream, d) if stream == 0 else has(stream, d) & (d > 0)

                @pl.when(here)
                def _():
                    for core in (0, 1):
                        b = block_of(stream, d, core)
                        relay_copy(b, j, way).wait_recv()

                        @pl.when(ring_next[way] != source)
                        def _():
                            relay_copy(b, j, way).start()

    steps = chunks * chips

    def body(step, carry):
        @pl.when(step < steps)
        def _():
            line_part(step)

        for way in (0, 1):
            late = step - LAG * hops[way]

            @pl.when((late >= 0) & (late < steps))
            def _():
                ring_part(late, way)

        return carry

    lax.fori_loop(0, chunks, body, 0)
    for copy in small:
        copy.wait()
    capacity, (depth, slots) = x_ref.shape[0], choose_ref.shape
    place_of = slot_target(counts_ref, (1, slots), 1, capacity)
    choose = (lax.broadcasted_iota(jnp.int32, (depth, slots), 0) == place_of).astype(jnp.float32)
    gap = pick(cond_band, cond_energy) - pick(val_band, val_energy)
    gap = lax.dot_general(
        gap, choose, (((1,), (1,)), ((), ())), precision=lax.Precision.HIGHEST, preferred_element_type=jnp.float32
    )
    for f in range(weights_ref.shape[0]):
        weights_ref[f] = -4.0 * gap / (gap * gap + freq_ref[f] * freq_ref[f])
    choose_ref[...] = choose.astype(jnp.bfloat16)
    lax.fori_loop(chunks, steps + LAG * (cols - 1), body, 0)

    def finish(step, carry):
        d, j = step // chunks, step % chunks
        for stream in (0, 1):
            here = has(stream, d) if stream == 0 else has(stream, d) & (d > 0)
            b = block_of(stream, d, k)
            theirs = block_of(stream, d, 1 - k)

            @pl.when(has(stream, d) & onward(stream))
            def _():
                line_copy(stream, d, j, b).wait_send()

            @pl.when(here)
            def _():
                mate_copy(b, j).wait_send()
                mate_copy(theirs, j).wait_recv()

                @pl.when(feeds(j))
                def _():
                    for way in (0, 1):
                        enter_copy(b, j, way).wait_send()

                @pl.when(relays(j))
                def _():
                    for core in (0, 1):
                        e = block_of(stream, d, core)
                        for way in (0, 1):
                            @pl.when(ring_next[way] != source)
                            def _():
                                relay_copy(e, j, way).wait_send()

        return carry

    lax.fori_loop(0, steps, finish, 0)

    @pl.when(source == c)
    def _():
        here = pltpu.make_async_copy(cols_ref.at[:, pl.ds((r % ratio) * 2 * halves, 2 * halves)], seg_ref, own_sem.at[0])
        here.start()
        here.wait()


def gather(x, counts, frequency, val_band, cond_band, val_energy, cond_energy, rows, cols):
    capacity, width = x.shape
    slots = rows * capacity
    live = slots * 5 // 8
    depth = pl.cdiv(live, 256) * 256
    ratio = rows // cols
    seg_width = width // ratio
    halves = 2 if seg_width % 512 == 0 else 1
    chunks, chips = ratio * halves, rows // 2
    dma = pltpu.SemaphoreType.DMA
    room = 2 * (slots * (width + seg_width) + depth * slots) + 4 * 8 * depth * frequency.shape[0]
    return pl.pallas_call(
        functools.partial(gather_kernel, rows, cols, halves),
        out_shape=(
            pltpu.VMEM((rows, 2 * chunks, capacity, seg_width // halves // 2), x.dtype),
            pltpu.VMEM((rows, 2 * halves, capacity, seg_width // halves // 2), x.dtype),
            pltpu.VMEM((depth, slots), jnp.bfloat16),
            pltpu.VMEM((frequency.shape[0], 8, depth), jnp.float32),
        ),
        in_specs=[pl.BlockSpec(memory_space=pl.ANY)] * 7,
        out_specs=[pl.BlockSpec(memory_space=pltpu.VMEM)] * 4,
        scratch_shapes=[
            pltpu.SMEM(counts.shape, counts.dtype),
            pltpu.SMEM(frequency.shape, frequency.dtype),
            pltpu.VMEM(val_band.shape, val_band.dtype),
            pltpu.VMEM(cond_band.shape, cond_band.dtype),
            pltpu.VMEM(val_energy.shape, val_energy.dtype),
            pltpu.VMEM(cond_energy.shape, cond_energy.dtype),
            dma((6,)),
            dma((2 * chunks,)),
            dma((2, chips, chunks)),
            dma((2, chips, chunks)),
            dma((rows, chunks)),
            dma((rows, chunks)),
            dma((rows, chunks, 2)),
            dma((rows, halves, 2)),
            dma((rows, halves, 2)),
        ],
        compiler_params=pltpu.CompilerParams(
            collective_id=0, has_side_effects=True, vmem_limit_bytes=VMEM - room - SPARE
        ),
    )(x, counts, frequency, val_band, cond_band, val_energy, cond_energy)


def exact_dot(a, b):
    return lax.dot_general(
        a, b, (((1,), (0,)), ((), ())), precision=lax.Precision.HIGHEST, preferred_element_type=jnp.float32
    )


def pick(band_ref, table_ref):
    levels, slots = table_ref.shape[0], band_ref.shape[0]
    hit = lax.broadcasted_iota(jnp.int32, (levels, slots), 0) == band_ref[...][None, :]
    return exact_dot(jnp.broadcast_to(table_ref[...][None, :], (8, levels)), hit.astype(jnp.float32))


def slot_target(counts_ref, shape, axis, capacity):
    slot = lax.broadcasted_iota(jnp.int32, shape, axis)
    target = jnp.full(shape, -1, jnp.int32)
    before = 0
    for block in range(counts_ref.shape[0]):
        inside = slot - block * capacity
        live = (inside >= 0) & (inside < counts_ref[block])
        target = jnp.where(live, inside + before, target)
        before = before + counts_ref[block]
    return target


def product_kernel(weights, choose_ref, seg_ref, cols_ref, out_ref, packed, turned, scaled):
    which, n = pl.program_id(0), pl.program_id(1)
    tile = out_ref.shape[2]
    rows, pieces, capacity, lane = cols_ref.shape
    slots = rows * capacity

    @pl.when((n == 0) & (which == 0))
    def _():
        choose = choose_ref[...]
        for p in range(pieces):
            piece = cols_ref[:, p].reshape(slots, lane)
            packed[:, p * lane : (p + 1) * lane] = jnp.dot(
                choose, piece, preferred_element_type=jnp.float32
            ).astype(jnp.bfloat16)
        for p in range(seg_ref.shape[1]):
            piece = seg_ref[:, p].reshape(slots, lane)
            turned[p * lane : (p + 1) * lane, :] = lax.dot_general(
                piece, choose, (((0,), (1,)), ((), ())), preferred_element_type=jnp.float32
            ).astype(jnp.bfloat16)

    @pl.when(n == 0)
    def _():
        scaled[...] = (turned[...].astype(jnp.float32) * weights[which][:1]).astype(jnp.bfloat16)

    start = pl.multiple_of(n * tile, tile)
    out_ref[0] = jnp.dot(scaled[...], packed[:, pl.ds(start, tile)], preferred_element_type=jnp.float32)


def product(weights, choose, seg, columns):
    freqs = weights.shape[0]
    rows, pieces, capacity, lane = columns.shape
    width, seg_width = pieces * lane, seg.shape[1] * lane
    depth = choose.shape[0]
    tile = math.gcd(width, TILE)
    vmem = pl.BlockSpec(memory_space=pltpu.VMEM)
    return pl.pallas_call(
        product_kernel,
        out_shape=jax.ShapeDtypeStruct((freqs, seg_width, width), jnp.float32),
        grid=(freqs, width // tile),
        in_specs=[vmem] * 4,
        out_specs=pl.BlockSpec((1, seg_width, tile), lambda f, n: (f, 0, n)),
        scratch_shapes=[
            pltpu.VMEM((depth, width), jnp.bfloat16),
            pltpu.VMEM((seg_width, depth), jnp.bfloat16),
            pltpu.VMEM((seg_width, depth), jnp.bfloat16),
        ],
        compiler_params=pltpu.CompilerParams(vmem_limit_bytes=40 * 1024 * 1024),
    )(weights, choose, seg, columns)


def plane_gather_kernel(rows, cols, x_ref, counts_hbm, freq_hbm, val_band_hbm, cond_band_hbm, val_energy_hbm,
                        cond_energy_hbm, packed_ref, seg_ref, choose_ref, weights_ref, cols_ref, counts_ref, freq_ref,
                        val_band, cond_band, val_energy, cond_energy, small_sem, own_sem, line_send, line_recv, mate_send,
                        mate_recv, enter_send, relay_send, seg_recv):
    r, c = lax.axis_index("row"), lax.axis_index("col")
    chips = rows // 2
    q, k = r // 2, r % 2
    pieces, lane = cols_ref.shape[1], cols_ref.shape[3]
    half = pieces // 2
    place = ring_place(c, cols)
    rel = (place - ring_place(q, cols) + cols) % cols
    near = [ring_place((place + 1) % cols, cols), ring_place((place + cols - 1) % cols, cols)]
    is_source = rel == 0
    up_ok, down_ok = q + 1 < chips, q >= 1
    lag = jnp.where(up_ok & down_ok, MIDDLE_LAG, END_LAG)

    own = [
        pltpu.make_async_copy(x_ref.at[:, pl.ds(p * lane, lane)], cols_ref.at[r, p], own_sem.at[p])
        for p in range(pieces)
    ]
    small = [
        pltpu.make_async_copy(src, dst, small_sem.at[i])
        for i, (src, dst) in enumerate((
            (counts_hbm, counts_ref), (freq_hbm, freq_ref), (val_band_hbm, val_band), (cond_band_hbm, cond_band),
            (val_energy_hbm, val_energy), (cond_energy_hbm, cond_energy),
        ))
    ]
    for copy in own + small:
        copy.start()
    barrier = pltpu.get_barrier_semaphore()

    def greet(row, col):
        pl.semaphore_signal(barrier, inc=1, device_id=(row, col), device_id_type=MESH)

    mate = 2 * q + 1 - k
    greet(mate, c)
    for nxt in near:
        greet(2 * q, nxt)
        greet(2 * q + 1, nxt)

    @pl.when(up_ok)
    def _():
        greet(r + 2, c)

    @pl.when(down_ok)
    def _():
        greet(r - 2, c)

    pl.semaphore_wait(barrier, 5 + up_ok.astype(jnp.int32) + down_ok.astype(jnp.int32))
    for copy in own:
        copy.wait()

    def remote(src, dst, send, recv, row, col):
        return pltpu.make_async_remote_copy(
            src_ref=src, dst_ref=dst, send_sem=send, recv_sem=recv, device_id=(row, col), device_id_type=MESH
        )

    def block_of(stream, d, core):
        return 2 * (q - d if stream == 0 else q + d) + core

    def has(stream, d):
        return q >= d if stream == 0 else q + d < chips

    def here(stream, d):
        return has(stream, d) if stream == 0 else has(stream, d) & (d > 0)

    def onward(stream):
        return up_ok if stream == 0 else down_ok

    def line_copy(stream, d, piece, arrival):
        row = r + 2 if stream == 0 else r - 2
        return remote(piece, piece, line_send.at[stream, d], arrival, row, c)

    def mate_copy(b, piece):
        return remote(piece, piece, mate_send.at[b], mate_recv.at[b], mate, c)

    def enter_copy(b, p, way):
        arrival = seg_recv.at[b, jnp.where(p % 2 == way, p % half, half)]
        return remote(cols_ref.at[b, p], seg_ref.at[b, p % half], enter_send.at[b], arrival, 2 * q + p // half, near[way])

    def relay_copy(d, b, p, way):
        last = (rel == 2) | tree(d)
        piece = seg_ref.at[b, p % half]
        return remote(piece, piece, relay_send.at[b], seg_recv.at[b, jnp.where(last, half, p % half)], r, near[way])

    def await_sends(ref, sem):
        remote(ref, ref, sem, mate_recv.at[0], mate, c).wait_send()

    def await_arrivals(ref, sem):
        remote(ref, ref, mate_send.at[0], sem, mate, c).wait_recv()

    def tree(d):
        return d == chips - 1

    def enters(d, p, way):
        return (p % 2 == way) | tree(d)

    def forwards(d, p, way):
        return (p % 2 == way) & ((rel == (1 if way == 0 else cols - 1)) | ((rel == 2) & ~tree(d)))

    def feed(d, p, b):
        @pl.when(is_source)
        def _():
            for way in (0, 1):
                @pl.when(enters(d, p, way))
                def _():
                    enter_copy(b, p, way).start()

    def begin(p, carry):
        for stream in (0, 1):
            @pl.when(onward(stream))
            def _():
                line_copy(stream, 0, cols_ref.at[r, p], line_recv.at[stream, 0, p]).start()

        feed(0, p, r)
        mate_copy(r, cols_ref.at[r, p]).start()
        return carry

    lax.fori_loop(0, pieces, begin, 0)

    for copy in small:
        copy.wait()
    capacity, (depth, slots) = x_ref.shape[0], choose_ref.shape
    place_of = slot_target(counts_ref, (1, slots), 1, capacity)
    choose = (lax.broadcasted_iota(jnp.int32, (depth, slots), 0) == place_of).astype(jnp.float32)
    gap = pick(cond_band, cond_energy) - pick(val_band, val_energy)
    gap = lax.dot_general(
        gap, choose, (((1,), (1,)), ((), ())), precision=lax.Precision.HIGHEST, preferred_element_type=jnp.float32
    )
    for f in range(weights_ref.shape[0]):
        weights_ref[f] = -4.0 * gap / (gap * gap + freq_ref[f] * freq_ref[f])
    choose_ref[...] = choose.astype(jnp.bfloat16)

    def line_part(step):
        d, p = step // pieces + 1, step % pieces
        for stream in (0, 1):
            b = block_of(stream, d, k)

            @pl.when(has(stream, d))
            def _():
                piece = cols_ref.at[b, p]
                await_arrivals(piece, line_recv.at[stream, d - 1, p])

                @pl.when(onward(stream))
                def _():
                    line_copy(stream, d, piece, line_recv.at[stream, d, p]).start()

                feed(d, p, b)
                mate_copy(b, piece).start()

    def relay_part(step, way):
        d, p = step // pieces, step % pieces

        @pl.when((p // half == k) & forwards(d, p, way))
        def _():
            for stream in (0, 1):
                @pl.when(here(stream, d))
                def _():
                    for core in (0, 1):
                        b = block_of(stream, d, core)
                        await_arrivals(seg_ref.at[b, p % half], seg_recv.at[b, p % half])
                        relay_copy(d, b, p, way).start()

    steps = pieces * (chips - 1)
    delay = lag * jnp.where(rel == 2, 2, 1)

    def body(step, carry):
        @pl.when((step >= 0) & (step < steps))
        def _():
            line_part(step)

        late = step - delay + pieces
        for way in (0, 1):
            @pl.when((late >= 0) & (late < steps + pieces))
            def _():
                relay_part(late, way)

        return carry

    lax.fori_loop(jnp.minimum(delay - pieces, 0), steps + delay, body, 0)

    def gather_end(d, carry):
        for stream in (0, 1):
            @pl.when(here(stream, d))
            def _():
                b = block_of(stream, d, 1 - k)
                await_arrivals(cols_ref.at[b], mate_recv.at[b])

        return carry

    lax.fori_loop(0, chips, gather_end, 0)
    stay = pltpu.make_async_copy(cols_ref.at[:, pl.ds(k * half, half)], seg_ref, own_sem.at[0])

    @pl.when(is_source)
    def _():
        stay.start()

    choice = choose_ref[...]
    for p in range(pieces):
        piece = cols_ref[:, p].reshape(slots, lane)
        packed_ref[:, p * lane : (p + 1) * lane] = jnp.dot(
            choice, piece, preferred_element_type=jnp.float32
        ).astype(jnp.bfloat16)

    def finish(d, carry):
        for stream in (0, 1):
            b = block_of(stream, d, k)

            @pl.when(has(stream, d) & onward(stream))
            def _():
                await_sends(cols_ref.at[b], line_send.at[stream, d])

            @pl.when(here(stream, d))
            def _():
                await_sends(cols_ref.at[b], mate_send.at[b])

                @pl.when(is_source & tree(d))
                def _():
                    await_sends(cols_ref.at[pl.ds(0, 2)], enter_send.at[b])

                @pl.when(is_source & ~tree(d))
                def _():
                    await_sends(cols_ref.at[b], enter_send.at[b])

                for core in (0, 1):
                    e = block_of(stream, d, core)

                    @pl.when((rel == 1) | (rel == cols - 1))
                    def _():
                        await_sends(seg_ref.at[e, pl.ds(0, half // 2)], relay_send.at[e])
                        await_arrivals(seg_ref.at[e, pl.ds(0, half // 2)], seg_recv.at[e, half])

                    @pl.when((rel == 2) & ~tree(d))
                    def _():
                        await_sends(seg_ref.at[e], relay_send.at[e])

                    @pl.when((rel == 2) & tree(d))
                    def _():
                        await_arrivals(seg_ref.at[e], seg_recv.at[e, half])

        return carry

    lax.fori_loop(0, chips, finish, 0)

    @pl.when(is_source)
    def _():
        stay.wait()


def plane_gather(x, counts, frequency, val_band, cond_band, val_energy, cond_energy, rows, cols):
    capacity, width = x.shape
    slots = rows * capacity
    depth = pl.cdiv(slots * 5 // 8, 256) * 256
    chips, pieces = rows // 2, PIECES
    half, lane, freqs = pieces // 2, width // pieces, frequency.shape[0]
    dma = pltpu.SemaphoreType.DMA
    room = 2 * (slots * width // 2 + depth * (width + slots)) + 4 * 8 * depth * freqs
    return pl.pallas_call(
        functools.partial(plane_gather_kernel, rows, cols),
        out_shape=(
            pltpu.VMEM((depth, width), x.dtype),
            pltpu.VMEM((rows, half, capacity, lane), x.dtype),
            pltpu.VMEM((depth, slots), jnp.bfloat16),
            pltpu.VMEM((freqs, 8, depth), jnp.float32),
        ),
        in_specs=[pl.BlockSpec(memory_space=pl.ANY)] * 7,
        out_specs=[pl.BlockSpec(memory_space=pltpu.VMEM)] * 4,
        scratch_shapes=[
            pltpu.VMEM((rows, pieces, capacity, lane), x.dtype),
            pltpu.SMEM(counts.shape, counts.dtype),
            pltpu.SMEM(frequency.shape, frequency.dtype),
            pltpu.VMEM(val_band.shape, val_band.dtype),
            pltpu.VMEM(cond_band.shape, cond_band.dtype),
            pltpu.VMEM(val_energy.shape, val_energy.dtype),
            pltpu.VMEM(cond_energy.shape, cond_energy.dtype),
            dma((6,)),
            dma((pieces,)),
            dma((2, chips)),
            dma((2, chips, pieces)),
            dma((rows,)),
            dma((rows,)),
            dma((rows,)),
            dma((rows,)),
            dma((rows, half + 1)),
        ],
        compiler_params=pltpu.CompilerParams(
            collective_id=0, has_side_effects=True, vmem_limit_bytes=VMEM - room - SPARE
        ),
    )(x, counts, frequency, val_band, cond_band, val_energy, cond_energy)


def stream_kernel(weights, choose_ref, seg_ref, packed_ref, out_ref, turned, buf, sem):
    freqs, depth = weights.shape[0], choose_ref.shape[0]
    rows, chunks, capacity, lane = seg_ref.shape
    depth_slots = rows * capacity
    slots, part = buf.shape[0], buf.shape[2] // sem.shape[1]
    total = chunks * freqs

    def put(t, n):
        tall = pl.ds(pl.multiple_of((t // freqs) * lane, lane), lane)
        return pltpu.make_async_copy(
            buf.at[t % slots, :, pl.ds(n * part, part)],
            out_ref.at[t % freqs, tall, pl.ds(n * part, part)],
            sem.at[t % slots, n],
        )

    def body(t, carry):
        chunk, f = t // freqs, t % freqs

        @pl.when(f == 0)
        def _():
            piece = seg_ref[:, chunk].reshape(depth_slots, lane)
            turned[...] = lax.dot_general(
                piece, choose_ref[...], (((0,), (1,)), ((), ())), preferred_element_type=jnp.float32
            )

        scaled = (turned[...] * weights[f][:1]).astype(jnp.bfloat16)
        for n in range(sem.shape[1]):
            @pl.when(t >= slots)
            def _():
                put(t - slots, n).wait()

            buf[t % slots, :, n * part : (n + 1) * part] = jnp.dot(
                scaled, packed_ref[:, n * part : (n + 1) * part], preferred_element_type=jnp.float32
            )
            put(t, n).start()

        return carry

    lax.fori_loop(0, total, body, 0)

    def drain(t, carry):
        for n in range(sem.shape[1]):
            put(t, n).wait()
        return carry

    lax.fori_loop(max(total - slots, 0), total, drain, 0)


def stream_product(weights, choose, seg, packed):
    freqs = weights.shape[0]
    rows, chunks, capacity, lane = seg.shape
    depth, width = packed.shape
    parts = PARTS
    vmem = pl.BlockSpec(memory_space=pltpu.VMEM)
    return pl.pallas_call(
        stream_kernel,
        out_shape=jax.ShapeDtypeStruct((freqs, chunks * lane, width), jnp.float32),
        in_specs=[vmem] * 4,
        out_specs=pl.BlockSpec(memory_space=pl.ANY),
        scratch_shapes=[
            pltpu.VMEM((lane, depth), jnp.float32),
            pltpu.VMEM((BUFFERS, lane, width), jnp.float32),
            pltpu.SemaphoreType.DMA((BUFFERS, parts)),
        ],
        compiler_params=pltpu.CompilerParams(vmem_limit_bytes=40 * 1024 * 1024),
    )(weights, choose, seg, packed)


def per_device(pair_elems, counts, val_band, cond_band, val_energy, cond_energy, frequency):
    rows, cols = lax.axis_size("row"), lax.axis_size("col")
    if cols == 4 and rows == 2 * cols and pair_elems.shape[1] % (128 * PIECES) == 0:
        packed, seg, choose, weights = plane_gather(
            pair_elems, counts, frequency, val_band, cond_band, val_energy, cond_energy, rows, cols
        )
        return stream_product(weights, choose, seg, packed)
    columns, seg, choose, weights = gather(
        pair_elems, counts, frequency, val_band, cond_band, val_energy, cond_energy, rows, cols
    )
    return product(weights, choose, seg, columns)


def solution(mesh):
    in_specs = (P("row", "col"), P(), P(), P(), P(), P(), P())
    out_specs = P(None, "row", "col")
    return jax.shard_map(
        per_device, mesh=mesh, in_specs=in_specs, out_specs=out_specs, check_vma=False
    )
```

```python
import functools
import math

import jax
import jax.numpy as jnp
from jax import lax
from jax.experimental import pallas as pl
from jax.experimental.pallas import tpu as pltpu
from jax.sharding import PartitionSpec as P

MESH = pl.DeviceIdType.MESH
LAG = 3
TILE = 1024
VMEM = 67043328
SPARE = 1024 * 1024
PIECES = 8
PARTS = 2
FIRST_PARTS = 4
ROLE_DELAYS = {True: {False: (3, -1), True: (6, 2)}, False: {False: (8, 8), True: (16, 16)}}
HOLD_STEP = 3
SPREAD_STEP = 11


def ring_place(c, count):
    if count == 4:
        return c + (c // 2) * (1 - 2 * (c % 2))
    return c


def gather_kernel(rows, cols, halves, x_ref, counts_hbm, freq_hbm, val_band_hbm, cond_band_hbm, val_energy_hbm,
                  cond_energy_hbm, cols_ref, seg_ref, choose_ref, weights_ref, counts_ref, freq_ref, val_band, cond_band,
                  val_energy, cond_energy, small_sem, own_sem, line_send, line_recv, mate_send, mate_recv, enter_send,
                  relay_send, ring_recv):
    r, c = lax.axis_index("row"), lax.axis_index("col")
    chips = rows // 2
    q, k = r // 2, r % 2
    pieces, lane = cols_ref.shape[1], cols_ref.shape[3]
    ratio = rows // cols
    chunks = ratio * halves
    place = ring_place(c, cols)
    source = r // ratio
    ring_next = [ring_place((place + 1) % cols, cols), ring_place((place + cols - 1) % cols, cols)]
    ahead = (place - ring_place(source, cols) + cols) % cols
    hops = [ahead, cols - ahead]
    up_ok, down_ok = q + 1 < chips, q >= 1

    own = [
        pltpu.make_async_copy(x_ref.at[:, pl.ds(p * lane, lane)], cols_ref.at[r, p], own_sem.at[p])
        for p in range(pieces)
    ]
    small = [
        pltpu.make_async_copy(src, dst, small_sem.at[i])
        for i, (src, dst) in enumerate((
            (counts_hbm, counts_ref), (freq_hbm, freq_ref), (val_band_hbm, val_band), (cond_band_hbm, cond_band),
            (val_energy_hbm, val_energy), (cond_energy_hbm, cond_energy),
        ))
    ]
    for copy in own + small:
        copy.start()
    barrier = pltpu.get_barrier_semaphore()

    def greet(row, col):
        pl.semaphore_signal(barrier, inc=1, device_id=(row, col), device_id_type=MESH)

    mate = 2 * q + 1 - k
    greet(mate, c)
    for nxt in ring_next:
        greet(2 * q, nxt)
        greet(2 * q + 1, nxt)

    @pl.when(up_ok)
    def _():
        greet(r + 2, c)

    @pl.when(down_ok)
    def _():
        greet(r - 2, c)

    pl.semaphore_wait(barrier, 5 + up_ok.astype(jnp.int32) + down_ok.astype(jnp.int32))
    for copy in own:
        copy.wait()

    def remote(src, dst, send, recv, row, col):
        return pltpu.make_async_remote_copy(
            src_ref=src, dst_ref=dst, send_sem=send, recv_sem=recv, device_id=(row, col), device_id_type=MESH
        )

    def block_of(stream, d, core):
        return 2 * (q - d if stream == 0 else q + d) + core

    def has(stream, d):
        return q >= d if stream == 0 else q + d < chips

    def line_copy(stream, d, j, b):
        ref = cols_ref.at[b, pl.ds(2 * j, 2)]
        row = r + 2 if stream == 0 else r - 2
        return remote(ref, ref, line_send.at[stream, d, j], line_recv.at[stream, d, j], row, c)

    def line_arrival(stream, d, j, b):
        ref = cols_ref.at[b, pl.ds(2 * j, 2)]
        return remote(ref, ref, line_send.at[stream, d, j], line_recv.at[stream, d - 1, j], mate, c)

    def mate_copy(b, j):
        ref = cols_ref.at[b, pl.ds(2 * j, 2)]
        return remote(ref, ref, mate_send.at[b, j], mate_recv.at[b, j], mate, c)

    def enter_copy(b, j, way):
        g = c * ratio + j // halves
        src = cols_ref.at[b, 2 * j + way]
        dst = seg_ref.at[b, 2 * (j % halves) + way]
        return remote(src, dst, enter_send.at[b, j, way], ring_recv.at[b, j % halves, way], g, ring_next[way])

    def relay_copy(b, j, way):
        ref = seg_ref.at[b, 2 * (j % halves) + way]
        return remote(ref, ref, relay_send.at[b, j % halves, way], ring_recv.at[b, j % halves, way], r, ring_next[way])

    def feeds(j):
        return (c * ratio + j // halves) // 2 == q

    def relays(j):
        return (source != c) & (j // halves == r % ratio)

    def onward(stream):
        return up_ok if stream == 0 else down_ok

    def line_part(step):
        d, j = step // chunks, step % chunks
        for stream in (0, 1):
            here = has(stream, d) if stream == 0 else has(stream, d) & (d > 0)
            b = block_of(stream, d, k)

            @pl.when(has(stream, d))
            def _():
                @pl.when(d > 0)
                def _():
                    line_arrival(stream, d, j, b).wait_recv()

                @pl.when(onward(stream))
                def _():
                    line_copy(stream, d, j, b).start()

            @pl.when(here)
            def _():
                mate_copy(b, j).start()

                @pl.when(feeds(j))
                def _():
                    for way in (0, 1):
                        enter_copy(b, j, way).start()

    def ring_part(step, way):
        d, j = step // chunks, step % chunks

        @pl.when(relays(j))
        def _():
            for stream in (0, 1):
                here = has(stream, d) if stream == 0 else has(stream, d) & (d > 0)

                @pl.when(here)
                def _():
                    for core in (0, 1):
                        b = block_of(stream, d, core)
                        relay_copy(b, j, way).wait_recv()

                        @pl.when(ring_next[way] != source)
                        def _():
                            relay_copy(b, j, way).start()

    steps = chunks * chips

    def body(step, carry):
        @pl.when(step < steps)
        def _():
            line_part(step)

        for way in (0, 1):
            late = step - LAG * hops[way]

            @pl.when((late >= 0) & (late < steps))
            def _():
                ring_part(late, way)

        return carry

    lax.fori_loop(0, chunks, body, 0)
    for copy in small:
        copy.wait()
    capacity, (depth, slots) = x_ref.shape[0], choose_ref.shape
    place_of = slot_target(counts_ref, (1, slots), 1, capacity)
    choose = (lax.broadcasted_iota(jnp.int32, (depth, slots), 0) == place_of).astype(jnp.float32)
    gap = pick(cond_band, cond_energy) - pick(val_band, val_energy)
    gap = lax.dot_general(
        gap, choose, (((1,), (1,)), ((), ())), precision=lax.Precision.HIGHEST, preferred_element_type=jnp.float32
    )
    for f in range(weights_ref.shape[0]):
        weights_ref[f] = -4.0 * gap / (gap * gap + freq_ref[f] * freq_ref[f])
    choose_ref[...] = choose.astype(jnp.bfloat16)
    lax.fori_loop(chunks, steps + LAG * (cols - 1), body, 0)

    def finish(step, carry):
        d, j = step // chunks, step % chunks
        for stream in (0, 1):
            here = has(stream, d) if stream == 0 else has(stream, d) & (d > 0)
            b = block_of(stream, d, k)
            theirs = block_of(stream, d, 1 - k)

            @pl.when(has(stream, d) & onward(stream))
            def _():
                line_copy(stream, d, j, b).wait_send()

            @pl.when(here)
            def _():
                mate_copy(b, j).wait_send()
                mate_copy(theirs, j).wait_recv()

                @pl.when(feeds(j))
                def _():
                    for way in (0, 1):
                        enter_copy(b, j, way).wait_send()

                @pl.when(relays(j))
                def _():
                    for core in (0, 1):
                        e = block_of(stream, d, core)
                        for way in (0, 1):
                            @pl.when(ring_next[way] != source)
                            def _():
                                relay_copy(e, j, way).wait_send()

        return carry

    lax.fori_loop(0, steps, finish, 0)

    @pl.when(source == c)
    def _():
        here = pltpu.make_async_copy(cols_ref.at[:, pl.ds((r % ratio) * 2 * halves, 2 * halves)], seg_ref, own_sem.at[0])
        here.start()
        here.wait()


def gather(x, counts, frequency, val_band, cond_band, val_energy, cond_energy, rows, cols):
    capacity, width = x.shape
    slots = rows * capacity
    live = slots * 5 // 8
    depth = pl.cdiv(live, 256) * 256
    ratio = rows // cols
    seg_width = width // ratio
    halves = 2 if seg_width % 512 == 0 else 1
    chunks, chips = ratio * halves, rows // 2
    dma = pltpu.SemaphoreType.DMA
    room = 2 * (slots * (width + seg_width) + depth * slots) + 4 * 8 * depth * frequency.shape[0]
    return pl.pallas_call(
        functools.partial(gather_kernel, rows, cols, halves),
        out_shape=(
            pltpu.VMEM((rows, 2 * chunks, capacity, seg_width // halves // 2), x.dtype),
            pltpu.VMEM((rows, 2 * halves, capacity, seg_width // halves // 2), x.dtype),
            pltpu.VMEM((depth, slots), jnp.bfloat16),
            pltpu.VMEM((frequency.shape[0], 8, depth), jnp.float32),
        ),
        in_specs=[pl.BlockSpec(memory_space=pl.ANY)] * 7,
        out_specs=[pl.BlockSpec(memory_space=pltpu.VMEM)] * 4,
        scratch_shapes=[
            pltpu.SMEM(counts.shape, counts.dtype),
            pltpu.SMEM(frequency.shape, frequency.dtype),
            pltpu.VMEM(val_band.shape, val_band.dtype),
            pltpu.VMEM(cond_band.shape, cond_band.dtype),
            pltpu.VMEM(val_energy.shape, val_energy.dtype),
            pltpu.VMEM(cond_energy.shape, cond_energy.dtype),
            dma((6,)),
            dma((2 * chunks,)),
            dma((2, chips, chunks)),
            dma((2, chips, chunks)),
            dma((rows, chunks)),
            dma((rows, chunks)),
            dma((rows, chunks, 2)),
            dma((rows, halves, 2)),
            dma((rows, halves, 2)),
        ],
        compiler_params=pltpu.CompilerParams(
            collective_id=0, has_side_effects=True, vmem_limit_bytes=VMEM - room - SPARE
        ),
    )(x, counts, frequency, val_band, cond_band, val_energy, cond_energy)


def exact_dot(a, b):
    return lax.dot_general(
        a, b, (((1,), (0,)), ((), ())), precision=lax.Precision.HIGHEST, preferred_element_type=jnp.float32
    )


def pick(band_ref, table_ref):
    levels, slots = table_ref.shape[0], band_ref.shape[0]
    hit = lax.broadcasted_iota(jnp.int32, (levels, slots), 0) == band_ref[...][None, :]
    return exact_dot(jnp.broadcast_to(table_ref[...][None, :], (8, levels)), hit.astype(jnp.float32))


def slot_target(counts_ref, shape, axis, capacity):
    slot = lax.broadcasted_iota(jnp.int32, shape, axis)
    target = jnp.full(shape, -1, jnp.int32)
    before = 0
    for block in range(counts_ref.shape[0]):
        inside = slot - block * capacity
        live = (inside >= 0) & (inside < counts_ref[block])
        target = jnp.where(live, inside + before, target)
        before = before + counts_ref[block]
    return target


def product_kernel(weights, choose_ref, seg_ref, cols_ref, out_ref, packed, turned, scaled):
    which, n = pl.program_id(0), pl.program_id(1)
    tile = out_ref.shape[2]
    rows, pieces, capacity, lane = cols_ref.shape
    slots = rows * capacity

    @pl.when((n == 0) & (which == 0))
    def _():
        choose = choose_ref[...]
        for p in range(pieces):
            piece = cols_ref[:, p].reshape(slots, lane)
            packed[:, p * lane : (p + 1) * lane] = jnp.dot(
                choose, piece, preferred_element_type=jnp.float32
            ).astype(jnp.bfloat16)
        for p in range(seg_ref.shape[1]):
            piece = seg_ref[:, p].reshape(slots, lane)
            turned[p * lane : (p + 1) * lane, :] = lax.dot_general(
                piece, choose, (((0,), (1,)), ((), ())), preferred_element_type=jnp.float32
            ).astype(jnp.bfloat16)

    @pl.when(n == 0)
    def _():
        scaled[...] = (turned[...].astype(jnp.float32) * weights[which][:1]).astype(jnp.bfloat16)

    start = pl.multiple_of(n * tile, tile)
    out_ref[0] = jnp.dot(scaled[...], packed[:, pl.ds(start, tile)], preferred_element_type=jnp.float32)


def product(weights, choose, seg, columns):
    freqs = weights.shape[0]
    rows, pieces, capacity, lane = columns.shape
    width, seg_width = pieces * lane, seg.shape[1] * lane
    depth = choose.shape[0]
    tile = math.gcd(width, TILE)
    vmem = pl.BlockSpec(memory_space=pltpu.VMEM)
    return pl.pallas_call(
        product_kernel,
        out_shape=jax.ShapeDtypeStruct((freqs, seg_width, width), jnp.float32),
        grid=(freqs, width // tile),
        in_specs=[vmem] * 4,
        out_specs=pl.BlockSpec((1, seg_width, tile), lambda f, n: (f, 0, n)),
        scratch_shapes=[
            pltpu.VMEM((depth, width), jnp.bfloat16),
            pltpu.VMEM((seg_width, depth), jnp.bfloat16),
            pltpu.VMEM((seg_width, depth), jnp.bfloat16),
        ],
        compiler_params=pltpu.CompilerParams(vmem_limit_bytes=40 * 1024 * 1024),
    )(weights, choose, seg, columns)


def plane_gather_kernel(rows, cols, x_ref, counts_hbm, freq_hbm, val_band_hbm, cond_band_hbm, val_energy_hbm,
                        cond_energy_hbm, cols_ref, seg_ref, choose_ref, weights_ref, counts_ref, freq_ref,
                        val_band, cond_band, val_energy, cond_energy, small_sem, own_sem, line_send, line_recv, mate_send,
                        mate_recv, enter_send, relay_send, seg_recv, held, held_send, held_recv, aid_send,
                        aid_recv, aid_mate_send, aid_mate_recv):
    r, c = lax.axis_index("row"), lax.axis_index("col")
    chips = rows // 2
    q, k = r // 2, r % 2
    pieces, lane = cols_ref.shape[1], cols_ref.shape[3]
    half = pieces // 2
    place = ring_place(c, cols)
    rel = (place - ring_place(q, cols) + cols) % cols

    def chip_at(position):
        return ring_place((position + cols) % cols, cols)

    near = [chip_at(place + 1), chip_at(place - 1)]
    is_source = rel == 0
    up_ok, down_ok = q + 1 < chips, q >= 1
    end = ~(up_ok & down_ok)
    target = jnp.where(q == 1, 0, chips - 1)
    target_rel = (place - ring_place(target, cols) + cols) % cols
    helper = ((q == 1) | (q == chips - 2)) & ~end
    beside = jnp.where(q == 0, 1, chips - 2)
    aids = [(h * half + half // 2, cols - 1) for h in (0, 1)] + [(h * half + half // 2 + 1, 2) for h in (0, 1)]

    own = [
        pltpu.make_async_copy(x_ref.at[:, pl.ds(p * lane, lane)], cols_ref.at[r, p], own_sem.at[p])
        for p in range(pieces)
    ]
    small = [
        pltpu.make_async_copy(src, dst, small_sem.at[i])
        for i, (src, dst) in enumerate((
            (counts_hbm, counts_ref), (freq_hbm, freq_ref), (val_band_hbm, val_band), (cond_band_hbm, cond_band),
            (val_energy_hbm, val_energy), (cond_energy_hbm, cond_energy),
        ))
    ]
    for copy in own + small:
        copy.start()
    barrier = pltpu.get_barrier_semaphore()

    def greet(row, col):
        pl.semaphore_signal(barrier, inc=1, device_id=(row, col), device_id_type=MESH)

    mate = 2 * q + 1 - k
    greet(mate, c)
    for turn in range(1, cols):
        greet(r, chip_at(place + turn))

    @pl.when(is_source)
    def _():
        greet(mate, near[0])
        greet(mate, near[1])

    @pl.when(rel % 2 == 1)
    def _():
        greet(mate, chip_at(place - rel))

    @pl.when(up_ok)
    def _():
        greet(r + 2, c)

    @pl.when(down_ok)
    def _():
        greet(r - 2, c)

    crossing = (end & ~is_source) | (helper & (target_rel != 0))

    @pl.when(crossing)
    def _():
        greet(2 * jnp.where(end, beside, target) + 1 - k, c)

    calls = cols + jnp.where(is_source, 2, rel % 2) + (up_ok.astype(jnp.int32) + down_ok.astype(jnp.int32))
    pl.semaphore_wait(barrier, calls + crossing.astype(jnp.int32))
    for copy in own:
        copy.wait()

    def remote(src, dst, send, recv, row, col):
        return pltpu.make_async_remote_copy(
            src_ref=src, dst_ref=dst, send_sem=send, recv_sem=recv, device_id=(row, col), device_id_type=MESH
        )

    def block_of(stream, d, core):
        return 2 * (q - d if stream == 0 else q + d) + core

    def has(stream, d):
        return q >= d if stream == 0 else q + d < chips

    def here(stream, d):
        return has(stream, d) if stream == 0 else has(stream, d) & (d > 0)

    def onward(stream):
        return up_ok if stream == 0 else down_ok

    def line_copy(stream, d, piece, arrival):
        row = r + 2 if stream == 0 else r - 2
        return remote(piece, piece, line_send.at[stream, d], arrival, row, c)

    def mate_copy(b, piece):
        return remote(piece, piece, mate_send.at[b], mate_recv.at[b], mate, c)

    def enter_copy(b, p, way):
        arrival = seg_recv.at[b, jnp.where(p % 2 == way, p % half, half)]
        return remote(cols_ref.at[b, p], seg_ref.at[b, p % half], enter_send.at[b], arrival, 2 * q + p // half, near[way])

    def relay_copy(d, b, p, way):
        last = (rel == 2) | tree(d)
        piece = seg_ref.at[b, p % half]
        return remote(piece, piece, relay_send.at[b], seg_recv.at[b, jnp.where(last, half, p % half)], r, near[way])

    def await_sends(ref, sem):
        remote(ref, ref, sem, mate_recv.at[0], mate, c).wait_send()

    def await_arrivals(ref, sem):
        remote(ref, ref, mate_send.at[0], sem, mate, c).wait_recv()

    def tree(d):
        return d == jnp.maximum(q, chips - 1 - q)

    def aided(d, p):
        return end & (d == 1) & (p % half >= half // 2)

    def enters(d, p, way):
        return (p % 2 == way) | tree(d)

    def forwards(d, p, way):
        carries = (rel == (1 if way == 0 else cols - 1)) | ((rel == 2) & ~tree(d))
        return (p % 2 == way) & carries & ~aided(d, p)

    def held_copy(i, p, line):
        dst = held.at[i]
        return remote(cols_ref.at[r, p], dst, held_send, held_recv.at[i], r, chip_at(place + line))

    def aid_line_copy(i, p):
        b = r
        dst = seg_ref.at[b, p % half]
        return remote(held.at[i], dst, held_send, seg_recv.at[b, p % half], 2 * target + p // half, c)

    def aid_copy(b, p, turn):
        piece = seg_ref.at[b, p % half]
        return remote(piece, piece, aid_send, seg_recv.at[b, p % half], r, chip_at(place + turn))

    def aid_home_copy(i, core, b, p, line):
        return remote(seg_ref.at[b, p % half], cols_ref.at[b, p], aid_send, aid_recv.at[i, core], r, chip_at(place - line))

    def aid_mate_copy(b, p):
        piece = cols_ref.at[b, p]
        return remote(piece, piece, aid_mate_send, aid_mate_recv, mate, c)

    def feed(d, p, b):
        @pl.when(is_source)
        def _():
            for way in (0, 1):
                @pl.when(enters(d, p, way))
                def _():
                    enter_copy(b, p, way).start()

    def begin(p, carry):
        for stream in (0, 1):
            toward = target > q if stream == 0 else target < q
            spared = helper & (target_rel == 0) & toward & (p % half >= half // 2)

            @pl.when(onward(stream) & ~spared)
            def _():
                line_copy(stream, 0, cols_ref.at[r, p], line_recv.at[stream, 0, p]).start()

        feed(0, p, r)
        mate_copy(r, cols_ref.at[r, p]).start()
        return carry

    @pl.when(helper & (target_rel == 0))
    def _():
        for i, (p, line) in enumerate(aids):
            held_copy(i, p, line).start()

    lax.fori_loop(0, pieces, begin, 0)

    for copy in small:
        copy.wait()
    capacity, (depth, slots) = x_ref.shape[0], choose_ref.shape
    place_of = slot_target(counts_ref, (1, slots), 1, capacity)
    choose = (lax.broadcasted_iota(jnp.int32, (depth, slots), 0) == place_of).astype(jnp.float32)
    gap = pick(cond_band, cond_energy) - pick(val_band, val_energy)
    gap = lax.dot_general(
        gap, choose, (((1,), (1,)), ((), ())), precision=lax.Precision.HIGHEST, preferred_element_type=jnp.float32
    )
    for f in range(weights_ref.shape[0]):
        weights_ref[f] = -4.0 * gap / (gap * gap + freq_ref[f] * freq_ref[f])
    choose_ref[...] = choose.astype(jnp.bfloat16)

    def hold_part():
        for i, (p, line) in enumerate(aids):
            @pl.when(helper & (target_rel == line))
            def _():
                await_arrivals(held.at[i], held_recv.at[i])
                aid_line_copy(i, p).start()

    def spread_part():
        for i, (p, line) in enumerate(aids):
            @pl.when(end & (rel == line) & (k == p // half))
            def _():
                for core in (0, 1):
                    b = 2 * beside + core
                    await_arrivals(seg_ref.at[b, p % half], seg_recv.at[b, p % half])
                    aid_home_copy(i, core, b, p, line).start()
                    for turn in range(1, cols):
                        if (line + turn) % cols != 0:
                            aid_copy(b, p, turn).start()

    def land_part():
        for i, (p, line) in enumerate(aids):
            @pl.when(end & is_source & (k == p // half))
            def _():
                for core in (0, 1):
                    b = 2 * beside + core
                    await_arrivals(cols_ref.at[b, p], aid_recv.at[i, core])
                    aid_mate_copy(b, p).start()

    def line_step(d, p, ends, source):
        if ends:
            flow = jnp.where(q == 0, 1, 0)
            streams = [(flow, 2 * (q + jnp.where(q == 0, d, -d)) + k, None, (d > 0) & (d < chips))]
        else:
            streams = [
                (0, 2 * (q - d) + k, r + 2, (d > 0) & (d <= q)),
                (1, 2 * (q + d) + k, r - 2, (d > 0) & (d < chips - q)),
            ]
        for stream, b, row, present in streams:
            if ends and source and p % half >= half // 2:
                present = present & (d > 1)

            @pl.when(present)
            def _():
                piece = cols_ref.at[b, p]
                await_arrivals(piece, line_recv.at[stream, d - 1, p])
                if row is not None:
                    remote(piece, piece, line_send.at[stream, d], line_recv.at[stream, d, p], row, c).start()
                if source:
                    enter_copy(b, p, p % 2).start()

                    @pl.when(tree(d))
                    def _():
                        enter_copy(b, p, 1 - p % 2).start()

                mate_copy(b, piece).start()

    def relay_step(d, p, ends, opposite, least, most):
        mine = k == p // half
        if ends:
            blocks = [(2 * (q + jnp.where(q == 0, d, -d)), (d >= least) & (d <= most))]
            if p % half >= half // 2:
                mine = mine & (d != 1)
        else:
            blocks = [(2 * (q - d), (d >= least) & (d <= most) & (d <= q)), (2 * (q + d), (d >= least) & (d <= most) & (d > 0) & (d < chips - q))]
        if opposite:
            mine = mine & ~tree(d)
        else:
            mine = mine & (rel == (1 if p % 2 == 0 else cols - 1))

        @pl.when(mine)
        def _():
            for first, present in blocks:
                @pl.when(present)
                def _():
                    for core in (0, 1):
                        b = first + core
                        await_arrivals(seg_ref.at[b, p % half], seg_recv.at[b, p % half])
                        relay_copy(d, b, p, p % 2).start()

    def role(ends, place_in_ring):
        source, opposite = place_in_ring == 0, place_in_ring == 2
        near_delay, far_delay = ROLE_DELAYS[ends][opposite]

        def body(d, carry):
            for p in range(pieces):
                line_step(d, p, ends, source)
                step = d - 1
                if not ends and p == HOLD_STEP % pieces:
                    @pl.when(step == HOLD_STEP // pieces)
                    def _():
                        hold_part()

                if ends and not source and p == SPREAD_STEP % pieces:
                    @pl.when(step == SPREAD_STEP // pieces)
                    def _():
                        spread_part()

                if not source:
                    for delay, least, most in ((near_delay, 0, 1), (far_delay, 2, chips - 1)):
                        shift, late = divmod(p - delay, pieces)
                        relay_step(d + shift, late, ends, opposite, least, most)

            return carry

        turns = 0 if source else max(0, -(-max(near_delay, far_delay) // pieces))
        start = 1 if source else 0
        lax.fori_loop(start, chips + turns, body, 0)

    for ends in (False, True):
        for kind in (0, 1, 2):
            here_now = (rel == kind) if kind != 1 else (rel % 2 == 1)

            @pl.when(here_now & (end if ends else ~end))
            def _():
                role(ends, kind)

    @pl.when(end & is_source)
    def _():
        land_part()

    def gather_end(d, carry):
        for stream in (0, 1):
            @pl.when(here(stream, d))
            def _():
                b = block_of(stream, d, 1 - k)
                partial = is_source & aided(d, pieces - 1)

                @pl.when(partial)
                def _():
                    await_arrivals(cols_ref.at[b, pl.ds(0, half)], mate_recv.at[b])

                @pl.when(~partial)
                def _():
                    await_arrivals(cols_ref.at[b], mate_recv.at[b])

        return carry

    lax.fori_loop(0, chips, gather_end, 0)

    @pl.when(end & is_source)
    def _():
        await_arrivals(cols_ref.at[0, pl.ds(0, half)], aid_mate_recv)

    stay = pltpu.make_async_copy(cols_ref.at[:, pl.ds(k * half, half)], seg_ref, own_sem.at[0])

    @pl.when(is_source)
    def _():
        stay.start()

    def finish(d, carry):
        part = aided(d, pieces - 1)
        for stream in (0, 1):
            b = block_of(stream, d, k)
            toward = target > q if stream == 0 else target < q
            spared = helper & (target_rel == 0) & toward & (d == 0)

            @pl.when(has(stream, d) & onward(stream) & spared)
            def _():
                await_sends(cols_ref.at[b, pl.ds(0, half)], line_send.at[stream, d])

            @pl.when(has(stream, d) & onward(stream) & ~spared)
            def _():
                await_sends(cols_ref.at[b], line_send.at[stream, d])

            @pl.when(here(stream, d))
            def _():
                @pl.when(is_source & part)
                def _():
                    await_sends(cols_ref.at[b, pl.ds(0, half)], mate_send.at[b])
                    await_sends(cols_ref.at[b, pl.ds(0, half)], enter_send.at[b])

                @pl.when(~(is_source & part))
                def _():
                    await_sends(cols_ref.at[b], mate_send.at[b])

                @pl.when(is_source & tree(d))
                def _():
                    await_sends(cols_ref.at[pl.ds(0, 2)], enter_send.at[b])

                @pl.when(is_source & ~tree(d) & ~part)
                def _():
                    await_sends(cols_ref.at[b], enter_send.at[b])

                for core in (0, 1):
                    e = block_of(stream, d, core)
                    for some, count in ((part, half // 2), (~part, half)):
                        @pl.when(some & ((rel == 1) | (rel == cols - 1)))
                        def _():
                            await_sends(seg_ref.at[e, pl.ds(0, count // 2)], relay_send.at[e])
                            await_arrivals(seg_ref.at[e, pl.ds(0, count // 2)], seg_recv.at[e, half])

                        @pl.when(some & (rel == 2) & ~tree(d))
                        def _():
                            await_sends(seg_ref.at[e, pl.ds(0, count)], relay_send.at[e])

                    @pl.when((rel == 2) & tree(d))
                    def _():
                        await_arrivals(seg_ref.at[e], seg_recv.at[e, half])

        return carry

    for i, (p, line) in enumerate(aids):
        @pl.when(end & ~is_source & (rel != line) & (k == p // half))
        def _():
            for core in (0, 1):
                b = 2 * beside + core
                await_arrivals(seg_ref.at[b, p % half], seg_recv.at[b, p % half])

    for line in range(1, cols):
        for core in (0, 1):
            count = sum(1 for p, other in aids if other == line and p // half == core)
            if count > 0:
                @pl.when(end & (rel == line) & (k == core))
                def _():
                    await_sends(cols_ref.at[pl.ds(0, cols - 1), pl.ds(0, 2 * count)], aid_send)

    for line in range(1, cols):
        count = sum(1 for _, other in aids if other == line)
        if count > 0:
            @pl.when(helper & (target_rel == line))
            def _():
                await_sends(held.at[pl.ds(0, count)], held_send)

    @pl.when(helper & (target_rel == 0))
    def _():
        await_sends(held, held_send)

    @pl.when(end & is_source)
    def _():
        await_sends(cols_ref.at[0, pl.ds(0, half)], aid_mate_send)

    lax.fori_loop(0, chips, finish, 0)

    @pl.when(is_source)
    def _():
        stay.wait()


def plane_gather(x, counts, frequency, val_band, cond_band, val_energy, cond_energy, rows, cols):
    capacity, width = x.shape
    slots = rows * capacity
    depth = pl.cdiv(slots * 5 // 8, 256) * 256
    chips, pieces = rows // 2, PIECES
    half, lane, freqs = pieces // 2, width // pieces, frequency.shape[0]
    dma = pltpu.SemaphoreType.DMA
    room = 2 * (slots * width * 3 // 2 + depth * slots) + 4 * 8 * depth * freqs
    return pl.pallas_call(
        functools.partial(plane_gather_kernel, rows, cols),
        out_shape=(
            pltpu.VMEM((rows, pieces, capacity, lane), x.dtype),
            pltpu.VMEM((rows, half, capacity, lane), x.dtype),
            pltpu.VMEM((depth, slots), jnp.bfloat16),
            pltpu.VMEM((freqs, 8, depth), jnp.float32),
        ),
        in_specs=[pl.BlockSpec(memory_space=pl.ANY)] * 7,
        out_specs=[pl.BlockSpec(memory_space=pltpu.VMEM)] * 4,
        scratch_shapes=[
            pltpu.SMEM(counts.shape, counts.dtype),
            pltpu.SMEM(frequency.shape, frequency.dtype),
            pltpu.VMEM(val_band.shape, val_band.dtype),
            pltpu.VMEM(cond_band.shape, cond_band.dtype),
            pltpu.VMEM(val_energy.shape, val_energy.dtype),
            pltpu.VMEM(cond_energy.shape, cond_energy.dtype),
            dma((6,)),
            dma((pieces,)),
            dma((2, chips)),
            dma((2, chips, pieces)),
            dma((rows,)),
            dma((rows,)),
            dma((rows,)),
            dma((rows,)),
            dma((rows, half + 1)),
            pltpu.VMEM((half, capacity, lane), x.dtype),
            dma(()),
            dma((half,)),
            dma(()),
            dma((half, 2)),
            dma(()),
            dma(()),
        ],
        compiler_params=pltpu.CompilerParams(
            collective_id=0, has_side_effects=True, vmem_limit_bytes=VMEM - room - SPARE
        ),
    )(x, counts, frequency, val_band, cond_band, val_energy, cond_energy)


def stream_kernel(weights, choose_ref, seg_ref, cols_ref, out_ref, turned, packed, buf, sem):
    freqs = weights.shape[0]
    rows, chunks, capacity, lane = seg_ref.shape
    slots, width = rows * capacity, packed.shape[1]
    firsts, parts = sem.shape[1], PARTS
    first, part = width // firsts, width // parts
    group = first // lane

    def put(chunk, f, n, wide):
        tall = pl.ds(pl.multiple_of(chunk * lane, lane), lane)
        across = pl.ds(n * wide, wide)
        return pltpu.make_async_copy(buf.at[f, :, across], out_ref.at[f, tall, across], sem.at[f, n])

    def turn(chunk):
        turned[...] = lax.dot_general(
            seg_ref[:, chunk].reshape(slots, lane), choose_ref[...], (((0,), (1,)), ((), ())),
            preferred_element_type=jnp.float32,
        )

    def scale(f):
        return (turned[...] * weights[f][:1]).astype(jnp.bfloat16)

    turn(0)
    for n in range(firsts):
        across = pl.ds(n * first, first)
        for p in range(n * group, (n + 1) * group):
            packed[:, p * lane : (p + 1) * lane] = jnp.dot(
                choose_ref[...], cols_ref[:, p].reshape(slots, lane), preferred_element_type=jnp.float32
            ).astype(jnp.bfloat16)
        for f in range(freqs):
            buf[f, :, across] = jnp.dot(scale(f), packed[:, across], preferred_element_type=jnp.float32)
            put(0, f, n, first).start()

    def body(t, carry):
        chunk, f = t // freqs, t % freqs

        @pl.when(f == 0)
        def _():
            turn(chunk)

        scaled = scale(f)
        for n in range(parts):
            @pl.when(chunk == 1)
            def _():
                for m in range(n * firsts // parts, (n + 1) * firsts // parts):
                    put(0, f, m, first).wait()

            @pl.when(chunk > 1)
            def _():
                put(chunk - 1, f, n, part).wait()

            across = pl.ds(n * part, part)
            buf[f, :, across] = jnp.dot(scaled, packed[:, across], preferred_element_type=jnp.float32)
            put(chunk, f, n, part).start()

        return carry

    lax.fori_loop(freqs, chunks * freqs, body, 0)

    def drain(f, carry):
        for n in range(parts):
            put(chunks - 1, f, n, part).wait()
        return carry

    lax.fori_loop(0, freqs, drain, 0)


def stream_product(weights, choose, seg, columns):
    freqs = weights.shape[0]
    rows, chunks, capacity, lane = seg.shape
    width, depth = columns.shape[1] * lane, choose.shape[0]
    vmem = pl.BlockSpec(memory_space=pltpu.VMEM)
    return pl.pallas_call(
        stream_kernel,
        out_shape=jax.ShapeDtypeStruct((freqs, chunks * lane, width), jnp.float32),
        in_specs=[vmem] * 4,
        out_specs=pl.BlockSpec(memory_space=pl.ANY),
        scratch_shapes=[
            pltpu.VMEM((lane, depth), jnp.float32),
            pltpu.VMEM((depth, width), jnp.bfloat16),
            pltpu.VMEM((freqs, lane, width), jnp.float32),
            pltpu.SemaphoreType.DMA((freqs, FIRST_PARTS)),
        ],
        compiler_params=pltpu.CompilerParams(vmem_limit_bytes=40 * 1024 * 1024),
    )(weights, choose, seg, columns)


def per_device(pair_elems, counts, val_band, cond_band, val_energy, cond_energy, frequency):
    rows, cols = lax.axis_size("row"), lax.axis_size("col")
    if cols == 4 and rows == 2 * cols and pair_elems.shape[1] % (128 * PIECES) == 0:
        columns, seg, choose, weights = plane_gather(
            pair_elems, counts, frequency, val_band, cond_band, val_energy, cond_energy, rows, cols
        )
        return stream_product(weights, choose, seg, columns)
    columns, seg, choose, weights = gather(
        pair_elems, counts, frequency, val_band, cond_band, val_energy, cond_energy, rows, cols
    )
    return product(weights, choose, seg, columns)


def solution(mesh):
    in_specs = (P("row", "col"), P(), P(), P(), P(), P(), P())
    out_specs = P(None, "row", "col")
    return jax.shard_map(
        per_device, mesh=mesh, in_specs=in_specs, out_specs=out_specs, check_vma=False
    )
```

```python
import functools
import math

import jax
import jax.numpy as jnp
from jax import lax
from jax.experimental import pallas as pl
from jax.experimental.pallas import tpu as pltpu
from jax.sharding import PartitionSpec as P

MESH = pl.DeviceIdType.MESH
LAG = 3
TILE = 1024
VMEM = 67043328
SPARE = 1024 * 1024
PIECES = 8
PARTS = 2
FIRST_PARTS = 4
ROLE_DELAYS = {True: {False: (3, 0), True: (6, 3)}, False: {False: (7, 7), True: (14, 14)}}
HOLD_STEP = 0
SPREAD_STEP = 10


def ring_place(c, count):
    if count == 4:
        return c + (c // 2) * (1 - 2 * (c % 2))
    return c


def gather_kernel(rows, cols, halves, x_ref, counts_hbm, freq_hbm, val_band_hbm, cond_band_hbm, val_energy_hbm,
                  cond_energy_hbm, cols_ref, seg_ref, choose_ref, weights_ref, counts_ref, freq_ref, val_band, cond_band,
                  val_energy, cond_energy, small_sem, own_sem, line_send, line_recv, mate_send, mate_recv, enter_send,
                  relay_send, ring_recv):
    r, c = lax.axis_index("row"), lax.axis_index("col")
    chips = rows // 2
    q, k = r // 2, r % 2
    pieces, lane = cols_ref.shape[1], cols_ref.shape[3]
    ratio = rows // cols
    chunks = ratio * halves
    place = ring_place(c, cols)
    source = r // ratio
    ring_next = [ring_place((place + 1) % cols, cols), ring_place((place + cols - 1) % cols, cols)]
    ahead = (place - ring_place(source, cols) + cols) % cols
    hops = [ahead, cols - ahead]
    up_ok, down_ok = q + 1 < chips, q >= 1

    own = [
        pltpu.make_async_copy(x_ref.at[:, pl.ds(p * lane, lane)], cols_ref.at[r, p], own_sem.at[p])
        for p in range(pieces)
    ]
    small = [
        pltpu.make_async_copy(src, dst, small_sem.at[i])
        for i, (src, dst) in enumerate((
            (counts_hbm, counts_ref), (freq_hbm, freq_ref), (val_band_hbm, val_band), (cond_band_hbm, cond_band),
            (val_energy_hbm, val_energy), (cond_energy_hbm, cond_energy),
        ))
    ]
    for copy in own + small:
        copy.start()
    barrier = pltpu.get_barrier_semaphore()

    def greet(row, col):
        pl.semaphore_signal(barrier, inc=1, device_id=(row, col), device_id_type=MESH)

    mate = 2 * q + 1 - k
    greet(mate, c)
    for nxt in ring_next:
        greet(2 * q, nxt)
        greet(2 * q + 1, nxt)

    @pl.when(up_ok)
    def _():
        greet(r + 2, c)

    @pl.when(down_ok)
    def _():
        greet(r - 2, c)

    pl.semaphore_wait(barrier, 5 + up_ok.astype(jnp.int32) + down_ok.astype(jnp.int32))
    for copy in own:
        copy.wait()

    def remote(src, dst, send, recv, row, col):
        return pltpu.make_async_remote_copy(
            src_ref=src, dst_ref=dst, send_sem=send, recv_sem=recv, device_id=(row, col), device_id_type=MESH
        )

    def block_of(stream, d, core):
        return 2 * (q - d if stream == 0 else q + d) + core

    def has(stream, d):
        return q >= d if stream == 0 else q + d < chips

    def line_copy(stream, d, j, b):
        ref = cols_ref.at[b, pl.ds(2 * j, 2)]
        row = r + 2 if stream == 0 else r - 2
        return remote(ref, ref, line_send.at[stream, d, j], line_recv.at[stream, d, j], row, c)

    def line_arrival(stream, d, j, b):
        ref = cols_ref.at[b, pl.ds(2 * j, 2)]
        return remote(ref, ref, line_send.at[stream, d, j], line_recv.at[stream, d - 1, j], mate, c)

    def mate_copy(b, j):
        ref = cols_ref.at[b, pl.ds(2 * j, 2)]
        return remote(ref, ref, mate_send.at[b, j], mate_recv.at[b, j], mate, c)

    def enter_copy(b, j, way):
        g = c * ratio + j // halves
        src = cols_ref.at[b, 2 * j + way]
        dst = seg_ref.at[b, 2 * (j % halves) + way]
        return remote(src, dst, enter_send.at[b, j, way], ring_recv.at[b, j % halves, way], g, ring_next[way])

    def relay_copy(b, j, way):
        ref = seg_ref.at[b, 2 * (j % halves) + way]
        return remote(ref, ref, relay_send.at[b, j % halves, way], ring_recv.at[b, j % halves, way], r, ring_next[way])

    def feeds(j):
        return (c * ratio + j // halves) // 2 == q

    def relays(j):
        return (source != c) & (j // halves == r % ratio)

    def onward(stream):
        return up_ok if stream == 0 else down_ok

    def line_part(step):
        d, j = step // chunks, step % chunks
        for stream in (0, 1):
            here = has(stream, d) if stream == 0 else has(stream, d) & (d > 0)
            b = block_of(stream, d, k)

            @pl.when(has(stream, d))
            def _():
                @pl.when(d > 0)
                def _():
                    line_arrival(stream, d, j, b).wait_recv()

                @pl.when(onward(stream))
                def _():
                    line_copy(stream, d, j, b).start()

            @pl.when(here)
            def _():
                mate_copy(b, j).start()

                @pl.when(feeds(j))
                def _():
                    for way in (0, 1):
                        enter_copy(b, j, way).start()

    def ring_part(step, way):
        d, j = step // chunks, step % chunks

        @pl.when(relays(j))
        def _():
            for stream in (0, 1):
                here = has(stream, d) if stream == 0 else has(stream, d) & (d > 0)

                @pl.when(here)
                def _():
                    for core in (0, 1):
                        b = block_of(stream, d, core)
                        relay_copy(b, j, way).wait_recv()

                        @pl.when(ring_next[way] != source)
                        def _():
                            relay_copy(b, j, way).start()

    steps = chunks * chips

    def body(step, carry):
        @pl.when(step < steps)
        def _():
            line_part(step)

        for way in (0, 1):
            late = step - LAG * hops[way]

            @pl.when((late >= 0) & (late < steps))
            def _():
                ring_part(late, way)

        return carry

    lax.fori_loop(0, chunks, body, 0)
    for copy in small:
        copy.wait()
    capacity, (depth, slots) = x_ref.shape[0], choose_ref.shape
    place_of = slot_target(counts_ref, (1, slots), 1, capacity)
    choose = (lax.broadcasted_iota(jnp.int32, (depth, slots), 0) == place_of).astype(jnp.float32)
    gap = pick(cond_band, cond_energy) - pick(val_band, val_energy)
    gap = lax.dot_general(
        gap, choose, (((1,), (1,)), ((), ())), precision=lax.Precision.HIGHEST, preferred_element_type=jnp.float32
    )
    for f in range(weights_ref.shape[0]):
        weights_ref[f] = -4.0 * gap / (gap * gap + freq_ref[f] * freq_ref[f])
    choose_ref[...] = choose.astype(jnp.bfloat16)
    lax.fori_loop(chunks, steps + LAG * (cols - 1), body, 0)

    def finish(step, carry):
        d, j = step // chunks, step % chunks
        for stream in (0, 1):
            here = has(stream, d) if stream == 0 else has(stream, d) & (d > 0)
            b = block_of(stream, d, k)
            theirs = block_of(stream, d, 1 - k)

            @pl.when(has(stream, d) & onward(stream))
            def _():
                line_copy(stream, d, j, b).wait_send()

            @pl.when(here)
            def _():
                mate_copy(b, j).wait_send()
                mate_copy(theirs, j).wait_recv()

                @pl.when(feeds(j))
                def _():
                    for way in (0, 1):
                        enter_copy(b, j, way).wait_send()

                @pl.when(relays(j))
                def _():
                    for core in (0, 1):
                        e = block_of(stream, d, core)
                        for way in (0, 1):
                            @pl.when(ring_next[way] != source)
                            def _():
                                relay_copy(e, j, way).wait_send()

        return carry

    lax.fori_loop(0, steps, finish, 0)

    @pl.when(source == c)
    def _():
        here = pltpu.make_async_copy(cols_ref.at[:, pl.ds((r % ratio) * 2 * halves, 2 * halves)], seg_ref, own_sem.at[0])
        here.start()
        here.wait()


def gather(x, counts, frequency, val_band, cond_band, val_energy, cond_energy, rows, cols):
    capacity, width = x.shape
    slots = rows * capacity
    live = slots * 5 // 8
    depth = pl.cdiv(live, 256) * 256
    ratio = rows // cols
    seg_width = width // ratio
    halves = 2 if seg_width % 512 == 0 else 1
    chunks, chips = ratio * halves, rows // 2
    dma = pltpu.SemaphoreType.DMA
    room = 2 * (slots * (width + seg_width) + depth * slots) + 4 * 8 * depth * frequency.shape[0]
    return pl.pallas_call(
        functools.partial(gather_kernel, rows, cols, halves),
        out_shape=(
            pltpu.VMEM((rows, 2 * chunks, capacity, seg_width // halves // 2), x.dtype),
            pltpu.VMEM((rows, 2 * halves, capacity, seg_width // halves // 2), x.dtype),
            pltpu.VMEM((depth, slots), jnp.bfloat16),
            pltpu.VMEM((frequency.shape[0], 8, depth), jnp.float32),
        ),
        in_specs=[pl.BlockSpec(memory_space=pl.ANY)] * 7,
        out_specs=[pl.BlockSpec(memory_space=pltpu.VMEM)] * 4,
        scratch_shapes=[
            pltpu.SMEM(counts.shape, counts.dtype),
            pltpu.SMEM(frequency.shape, frequency.dtype),
            pltpu.VMEM(val_band.shape, val_band.dtype),
            pltpu.VMEM(cond_band.shape, cond_band.dtype),
            pltpu.VMEM(val_energy.shape, val_energy.dtype),
            pltpu.VMEM(cond_energy.shape, cond_energy.dtype),
            dma((6,)),
            dma((2 * chunks,)),
            dma((2, chips, chunks)),
            dma((2, chips, chunks)),
            dma((rows, chunks)),
            dma((rows, chunks)),
            dma((rows, chunks, 2)),
            dma((rows, halves, 2)),
            dma((rows, halves, 2)),
        ],
        compiler_params=pltpu.CompilerParams(
            collective_id=0, has_side_effects=True, vmem_limit_bytes=VMEM - room - SPARE
        ),
    )(x, counts, frequency, val_band, cond_band, val_energy, cond_energy)


def exact_dot(a, b):
    return lax.dot_general(
        a, b, (((1,), (0,)), ((), ())), precision=lax.Precision.HIGHEST, preferred_element_type=jnp.float32
    )


def pick(band_ref, table_ref):
    levels, slots = table_ref.shape[0], band_ref.shape[0]
    hit = lax.broadcasted_iota(jnp.int32, (levels, slots), 0) == band_ref[...][None, :]
    return exact_dot(jnp.broadcast_to(table_ref[...][None, :], (8, levels)), hit.astype(jnp.float32))


def slot_target(counts_ref, shape, axis, capacity):
    slot = lax.broadcasted_iota(jnp.int32, shape, axis)
    target = jnp.full(shape, -1, jnp.int32)
    before = 0
    for block in range(counts_ref.shape[0]):
        inside = slot - block * capacity
        live = (inside >= 0) & (inside < counts_ref[block])
        target = jnp.where(live, inside + before, target)
        before = before + counts_ref[block]
    return target


def product_kernel(weights, choose_ref, seg_ref, cols_ref, out_ref, packed, turned, scaled):
    which, n = pl.program_id(0), pl.program_id(1)
    tile = out_ref.shape[2]
    rows, pieces, capacity, lane = cols_ref.shape
    slots = rows * capacity

    @pl.when((n == 0) & (which == 0))
    def _():
        choose = choose_ref[...]
        for p in range(pieces):
            piece = cols_ref[:, p].reshape(slots, lane)
            packed[:, p * lane : (p + 1) * lane] = jnp.dot(
                choose, piece, preferred_element_type=jnp.float32
            ).astype(jnp.bfloat16)
        for p in range(seg_ref.shape[1]):
            piece = seg_ref[:, p].reshape(slots, lane)
            turned[p * lane : (p + 1) * lane, :] = lax.dot_general(
                piece, choose, (((0,), (1,)), ((), ())), preferred_element_type=jnp.float32
            ).astype(jnp.bfloat16)

    @pl.when(n == 0)
    def _():
        scaled[...] = (turned[...].astype(jnp.float32) * weights[which][:1]).astype(jnp.bfloat16)

    start = pl.multiple_of(n * tile, tile)
    out_ref[0] = jnp.dot(scaled[...], packed[:, pl.ds(start, tile)], preferred_element_type=jnp.float32)


def product(weights, choose, seg, columns):
    freqs = weights.shape[0]
    rows, pieces, capacity, lane = columns.shape
    width, seg_width = pieces * lane, seg.shape[1] * lane
    depth = choose.shape[0]
    tile = math.gcd(width, TILE)
    vmem = pl.BlockSpec(memory_space=pltpu.VMEM)
    return pl.pallas_call(
        product_kernel,
        out_shape=jax.ShapeDtypeStruct((freqs, seg_width, width), jnp.float32),
        grid=(freqs, width // tile),
        in_specs=[vmem] * 4,
        out_specs=pl.BlockSpec((1, seg_width, tile), lambda f, n: (f, 0, n)),
        scratch_shapes=[
            pltpu.VMEM((depth, width), jnp.bfloat16),
            pltpu.VMEM((seg_width, depth), jnp.bfloat16),
            pltpu.VMEM((seg_width, depth), jnp.bfloat16),
        ],
        compiler_params=pltpu.CompilerParams(vmem_limit_bytes=40 * 1024 * 1024),
    )(weights, choose, seg, columns)


def plane_gather_kernel(rows, cols, x_ref, counts_hbm, freq_hbm, val_band_hbm, cond_band_hbm, val_energy_hbm,
                        cond_energy_hbm, cols_ref, seg_ref, choose_ref, weights_ref, counts_ref, freq_ref,
                        val_band, cond_band, val_energy, cond_energy, small_sem, own_sem, line_send, line_recv, mate_send,
                        mate_recv, enter_send, relay_send, seg_recv, held, held_send, held_recv, direct_send, aid_send,
                        aid_recv, aid_mate_send, aid_mate_recv):
    r, c = lax.axis_index("row"), lax.axis_index("col")
    chips = rows // 2
    q, k = r // 2, r % 2
    pieces, lane = cols_ref.shape[1], cols_ref.shape[3]
    half = pieces // 2
    place = ring_place(c, cols)
    rel = (place - ring_place(q, cols) + cols) % cols

    def chip_at(position):
        return ring_place((position + cols) % cols, cols)

    near = [chip_at(place + 1), chip_at(place - 1)]
    is_source = rel == 0
    up_ok, down_ok = q + 1 < chips, q >= 1
    end = ~(up_ok & down_ok)
    target = jnp.where(q == 1, 0, chips - 1)
    target_rel = (place - ring_place(target, cols) + cols) % cols
    helper = ((q == 1) | (q == chips - 2)) & ~end
    beside = jnp.where(q == 0, 1, chips - 2)
    aids = [(h * half + half // 2, cols - 1) for h in (0, 1)] + [(h * half + half // 2 + 1, 2) for h in (0, 1)]

    own = [
        pltpu.make_async_copy(x_ref.at[:, pl.ds(p * lane, lane)], cols_ref.at[r, p], own_sem.at[p])
        for p in range(pieces)
    ]
    small = [
        pltpu.make_async_copy(src, dst, small_sem.at[i])
        for i, (src, dst) in enumerate((
            (counts_hbm, counts_ref), (freq_hbm, freq_ref), (val_band_hbm, val_band), (cond_band_hbm, cond_band),
            (val_energy_hbm, val_energy), (cond_energy_hbm, cond_energy),
        ))
    ]
    for copy in own + small:
        copy.start()
    barrier = pltpu.get_barrier_semaphore()

    def greet(row, col):
        pl.semaphore_signal(barrier, inc=1, device_id=(row, col), device_id_type=MESH)

    mate = 2 * q + 1 - k
    across = end | (target_rel % 2 == 0) | (rel % 2 == 0)

    @pl.when(across)
    def _():
        greet(r, chip_at(place + 2))

    crossing = (end & (rel >= 2)) | (helper & (target_rel >= 2))

    @pl.when(crossing)
    def _():
        greet(2 * jnp.where(end, beside, target) + 1 - k, c)

    @pl.when(up_ok)
    def _():
        greet(r + 2, c)

    @pl.when(down_ok)
    def _():
        greet(r - 2, c)

    @pl.when(is_source)
    def _():
        greet(mate, near[0])
        greet(mate, near[1])
        greet(mate, chip_at(place + 2))

    @pl.when(~is_source)
    def _():
        greet(mate, chip_at(place - rel))

    greet(r, near[0])
    greet(r, near[1])
    greet(mate, c)
    calls = 3 + jnp.where(is_source, 3, 1) + up_ok.astype(jnp.int32) + down_ok.astype(jnp.int32)
    pl.semaphore_wait(barrier, calls + across.astype(jnp.int32) + crossing.astype(jnp.int32))
    for copy in own:
        copy.wait()

    def remote(src, dst, send, recv, row, col):
        return pltpu.make_async_remote_copy(
            src_ref=src, dst_ref=dst, send_sem=send, recv_sem=recv, device_id=(row, col), device_id_type=MESH
        )

    def block_of(stream, d, core):
        return 2 * (q - d if stream == 0 else q + d) + core

    def has(stream, d):
        return q >= d if stream == 0 else q + d < chips

    def here(stream, d):
        return has(stream, d) if stream == 0 else has(stream, d) & (d > 0)

    def onward(stream):
        return up_ok if stream == 0 else down_ok

    def line_copy(stream, d, piece, arrival):
        row = r + 2 if stream == 0 else r - 2
        return remote(piece, piece, line_send.at[stream, d], arrival, row, c)

    def mate_copy(b, piece):
        return remote(piece, piece, mate_send.at[b], mate_recv.at[b], mate, c)

    def enter_copy(b, p, way):
        arrival = seg_recv.at[b, jnp.where(p % 2 == way, p % half, half)]
        return remote(cols_ref.at[b, p], seg_ref.at[b, p % half], enter_send.at[b], arrival, 2 * q + p // half, near[way])

    def direct_copy(b, p):
        arrival = seg_recv.at[b, half]
        return remote(cols_ref.at[b, p], seg_ref.at[b, p % half], direct_send, arrival, 2 * q + p // half, chip_at(place + 2))

    def relay_copy(d, b, p, way):
        last = (rel == 2) | tree(d)
        piece = seg_ref.at[b, p % half]
        return remote(piece, piece, relay_send.at[b], seg_recv.at[b, jnp.where(last, half, p % half)], r, near[way])

    def await_sends(ref, sem):
        remote(ref, ref, sem, mate_recv.at[0], mate, c).wait_send()

    def await_arrivals(ref, sem):
        remote(ref, ref, mate_send.at[0], sem, mate, c).wait_recv()

    def tree(d):
        return d == jnp.maximum(q, chips - 1 - q)

    def aided(d, p):
        return end & (d == 1) & (p % half >= half // 2)

    def enters(d, p, way):
        return (p % 2 == way) | tree(d)

    def forwards(d, p, way):
        carries = (rel == (1 if way == 0 else cols - 1)) | ((rel == 2) & ~tree(d))
        return (p % 2 == way) & carries & ~aided(d, p)

    def held_copy(i, p, line):
        dst = held.at[i]
        return remote(cols_ref.at[r, p], dst, held_send, held_recv.at[i], r, chip_at(place + line))

    def aid_line_copy(i, p):
        b = r
        dst = seg_ref.at[b, p % half]
        return remote(held.at[i], dst, held_send, seg_recv.at[b, p % half], 2 * target + p // half, c)

    def aid_copy(b, p, turn):
        piece = seg_ref.at[b, p % half]
        return remote(piece, piece, aid_send, seg_recv.at[b, p % half], r, chip_at(place + turn))

    def aid_home_copy(i, core, b, p, line):
        return remote(seg_ref.at[b, p % half], cols_ref.at[b, p], aid_send, aid_recv.at[i, core], r, chip_at(place - line))

    def aid_mate_copy(b, p):
        piece = cols_ref.at[b, p]
        return remote(piece, piece, aid_mate_send, aid_mate_recv, mate, c)

    def feed(d, p, b):
        @pl.when(is_source)
        def _():
            for way in (0, 1):
                @pl.when(enters(d, p, way))
                def _():
                    enter_copy(b, p, way).start()

    def begin(p, carry):
        for stream in (0, 1):
            toward = target > q if stream == 0 else target < q
            spared = helper & (target_rel == 0) & toward & (p % half >= half // 2)

            paired = helper & (target_rel != 0) & toward

            @pl.when(onward(stream) & ~spared & ~paired)
            def _():
                line_copy(stream, 0, cols_ref.at[r, p], line_recv.at[stream, 0, p]).start()

            @pl.when(onward(stream) & paired & (p % 2 == 1))
            def _():
                line_copy(stream, 0, cols_ref.at[r, pl.ds(p - 1, 2)], line_recv.at[stream, 0, p]).start()

        feed(0, p, r)
        mate_copy(r, cols_ref.at[r, p]).start()
        return carry

    @pl.when(helper & (target_rel == 0))
    def _():
        for i, (p, line) in enumerate(aids):
            held_copy(i, p, line).start()

    lax.fori_loop(0, pieces, begin, 0)

    for copy in small:
        copy.wait()
    capacity, (depth, slots) = x_ref.shape[0], choose_ref.shape
    place_of = slot_target(counts_ref, (1, slots), 1, capacity)
    choose = (lax.broadcasted_iota(jnp.int32, (depth, slots), 0) == place_of).astype(jnp.float32)
    gap = pick(cond_band, cond_energy) - pick(val_band, val_energy)
    gap = lax.dot_general(
        gap, choose, (((1,), (1,)), ((), ())), precision=lax.Precision.HIGHEST, preferred_element_type=jnp.float32
    )
    for f in range(weights_ref.shape[0]):
        weights_ref[f] = -4.0 * gap / (gap * gap + freq_ref[f] * freq_ref[f])
    choose_ref[...] = choose.astype(jnp.bfloat16)

    def hold_part():
        for i, (p, line) in enumerate(aids):
            @pl.when(helper & (target_rel == line))
            def _():
                await_arrivals(held.at[i], held_recv.at[i])
                aid_line_copy(i, p).start()

    def spread_part():
        for i, (p, line) in enumerate(aids):
            @pl.when(end & (rel == line) & (k == p // half))
            def _():
                for core in (0, 1):
                    b = 2 * beside + core
                    await_arrivals(seg_ref.at[b, p % half], seg_recv.at[b, p % half])
                    aid_home_copy(i, core, b, p, line).start()
                    for turn in range(1, cols):
                        if (line + turn) % cols != 0:
                            aid_copy(b, p, turn).start()

    def land_part():
        for i, (p, line) in enumerate(aids):
            @pl.when(end & is_source & (k == p // half))
            def _():
                for core in (0, 1):
                    b = 2 * beside + core
                    await_arrivals(cols_ref.at[b, p], aid_recv.at[i, core])
                    aid_mate_copy(b, p).start()

    def line_step(d, p, ends, source):
        if ends:
            flow = jnp.where(q == 0, 1, 0)
            streams = [(flow, 2 * (q + jnp.where(q == 0, d, -d)) + k, None, (d > 0) & (d < chips))]
        else:
            streams = [
                (0, 2 * (q - d) + k, r + 2, (d > 0) & (d <= q)),
                (1, 2 * (q + d) + k, r - 2, (d > 0) & (d < chips - q)),
            ]
        paired = ends and not source
        if paired and p % 2 == 0:
            return
        for stream, b, row, present in streams:
            if ends and source and p % half >= half // 2:
                present = present & (d > 1)

            @pl.when(present)
            def _():
                piece = cols_ref.at[b, pl.ds(p - 1, 2)] if paired else cols_ref.at[b, p]
                await_arrivals(piece, line_recv.at[stream, d - 1, p])
                if row is not None:
                    double = (target_rel != 0) & ((target > q) if stream == 0 else (target < q))

                    @pl.when(~double)
                    def _():
                        line_copy(stream, d, piece, line_recv.at[stream, d, p]).start()

                    if p % 2 == 1:
                        @pl.when(double)
                        def _():
                            line_copy(stream, d, cols_ref.at[b, pl.ds(p - 1, 2)], line_recv.at[stream, d, p]).start()

                if source:
                    @pl.when(tree(d))
                    def _():
                        if p == pieces - 1:
                            direct_copy(b, p).start()
                        enter_copy(b, p, 1 - p % 2).start()

                    enter_copy(b, p, p % 2).start()

                mate_copy(b, piece).start()

    def relay_step(d, p, ends, opposite, least, most):
        mine = k == p // half
        if ends:
            blocks = [(2 * (q + jnp.where(q == 0, d, -d)), (d >= least) & (d <= most))]
            if p % half >= half // 2:
                mine = mine & (d != 1)
        else:
            blocks = [(2 * (q - d), (d >= least) & (d <= most) & (d <= q)), (2 * (q + d), (d >= least) & (d <= most) & (d > 0) & (d < chips - q))]
        if opposite:
            mine = mine & ~tree(d)
        else:
            mine = mine & (rel == (1 if p % 2 == 0 else cols - 1))

        @pl.when(mine)
        def _():
            for first, present in blocks:
                @pl.when(present)
                def _():
                    for core in (0, 1):
                        b = first + core
                        await_arrivals(seg_ref.at[b, p % half], seg_recv.at[b, p % half])

                        @pl.when(~tree(d) | (p < pieces - 1))
                        def _():
                            relay_copy(d, b, p, p % 2).start()

    def role(ends, place_in_ring):
        source, opposite = place_in_ring == 0, place_in_ring == 2
        near_delay, far_delay = ROLE_DELAYS[ends][opposite]

        def body(d, carry):
            for p in range(pieces):
                line_step(d, p, ends, source)
                step = d - 1
                if not ends and p == HOLD_STEP % pieces:
                    @pl.when(step == HOLD_STEP // pieces)
                    def _():
                        hold_part()

                if ends and not source and p == SPREAD_STEP % pieces:
                    @pl.when(step == SPREAD_STEP // pieces)
                    def _():
                        spread_part()

                if not source:
                    for delay, least, most in ((near_delay, 0, 1), (far_delay, 2, chips - 1)):
                        shift, late = divmod(p - delay, pieces)
                        relay_step(d + shift, late, ends, opposite, least, most)

            return carry

        turns = 0 if source else max(0, -(-max(near_delay, far_delay) // pieces))
        start = 1 if source else 0
        lax.fori_loop(start, chips + turns, body, 0)

    for ends in (False, True):
        for kind in (0, 1, 2):
            here_now = (rel == kind) if kind != 1 else (rel % 2 == 1)

            @pl.when(here_now & (end if ends else ~end))
            def _():
                role(ends, kind)

    @pl.when(end & is_source)
    def _():
        land_part()

    def gather_end(d, carry):
        for stream in (0, 1):
            @pl.when(here(stream, d))
            def _():
                b = block_of(stream, d, 1 - k)
                partial = is_source & aided(d, pieces - 1)

                @pl.when(partial)
                def _():
                    await_arrivals(cols_ref.at[b, pl.ds(0, half)], mate_recv.at[b])

                @pl.when(~partial)
                def _():
                    await_arrivals(cols_ref.at[b], mate_recv.at[b])

        return carry

    lax.fori_loop(0, chips, gather_end, 0)

    @pl.when(end & is_source)
    def _():
        await_arrivals(cols_ref.at[0, pl.ds(0, half)], aid_mate_recv)

    stay = pltpu.make_async_copy(cols_ref.at[:, pl.ds(k * half, half)], seg_ref, own_sem.at[0])

    @pl.when(is_source)
    def _():
        stay.start()

    def finish(d, carry):
        part = aided(d, pieces - 1)
        for stream in (0, 1):
            b = block_of(stream, d, k)
            toward = target > q if stream == 0 else target < q
            spared = helper & (target_rel == 0) & toward & (d == 0)

            @pl.when(has(stream, d) & onward(stream) & spared)
            def _():
                await_sends(cols_ref.at[b, pl.ds(0, half)], line_send.at[stream, d])

            @pl.when(has(stream, d) & onward(stream) & ~spared)
            def _():
                await_sends(cols_ref.at[b], line_send.at[stream, d])

            @pl.when(here(stream, d))
            def _():
                @pl.when(is_source & part)
                def _():
                    await_sends(cols_ref.at[b, pl.ds(0, half)], mate_send.at[b])
                    await_sends(cols_ref.at[b, pl.ds(0, half)], enter_send.at[b])

                @pl.when(~(is_source & part))
                def _():
                    await_sends(cols_ref.at[b], mate_send.at[b])

                @pl.when(is_source & tree(d))
                def _():
                    await_sends(cols_ref.at[pl.ds(0, 2)], enter_send.at[b])
                    await_sends(cols_ref.at[b, 0], direct_send)

                @pl.when(is_source & ~tree(d) & ~part)
                def _():
                    await_sends(cols_ref.at[b], enter_send.at[b])

                for core in (0, 1):
                    e = block_of(stream, d, core)
                    for some, count in ((part, half // 2), (~part, half)):
                        @pl.when(some & ((rel == 1) | (rel == cols - 1)))
                        def _():
                            fewer = (rel == cols - 1) & tree(d) & (k == 1)

                            @pl.when(fewer)
                            def _():
                                await_sends(seg_ref.at[e, pl.ds(0, max(count // 2 - 1, 1))], relay_send.at[e])

                            @pl.when(~fewer)
                            def _():
                                await_sends(seg_ref.at[e, pl.ds(0, count // 2)], relay_send.at[e])

                            await_arrivals(seg_ref.at[e, pl.ds(0, count // 2)], seg_recv.at[e, half])

                        @pl.when(some & (rel == 2) & ~tree(d))
                        def _():
                            await_sends(seg_ref.at[e, pl.ds(0, count)], relay_send.at[e])

                    @pl.when((rel == 2) & tree(d))
                    def _():
                        await_arrivals(seg_ref.at[e], seg_recv.at[e, half])

        return carry

    for i, (p, line) in enumerate(aids):
        @pl.when(end & ~is_source & (rel != line) & (k == p // half))
        def _():
            for core in (0, 1):
                b = 2 * beside + core
                await_arrivals(seg_ref.at[b, p % half], seg_recv.at[b, p % half])

    for line in range(1, cols):
        for core in (0, 1):
            count = sum(1 for p, other in aids if other == line and p // half == core)
            if count > 0:
                @pl.when(end & (rel == line) & (k == core))
                def _():
                    await_sends(cols_ref.at[pl.ds(0, cols - 1), pl.ds(0, 2 * count)], aid_send)

    for line in range(1, cols):
        count = sum(1 for _, other in aids if other == line)
        if count > 0:
            @pl.when(helper & (target_rel == line))
            def _():
                await_sends(held.at[pl.ds(0, count)], held_send)

    @pl.when(helper & (target_rel == 0))
    def _():
        await_sends(held, held_send)

    @pl.when(end & is_source)
    def _():
        await_sends(cols_ref.at[0, pl.ds(0, half)], aid_mate_send)

    lax.fori_loop(0, chips, finish, 0)

    @pl.when(is_source)
    def _():
        stay.wait()


def plane_gather(x, counts, frequency, val_band, cond_band, val_energy, cond_energy, rows, cols):
    capacity, width = x.shape
    slots = rows * capacity
    depth = pl.cdiv(slots * 5 // 8, 256) * 256
    chips, pieces = rows // 2, PIECES
    half, lane, freqs = pieces // 2, width // pieces, frequency.shape[0]
    dma = pltpu.SemaphoreType.DMA
    room = 2 * (slots * width * 3 // 2 + depth * slots) + 4 * 8 * depth * freqs
    return pl.pallas_call(
        functools.partial(plane_gather_kernel, rows, cols),
        out_shape=(
            pltpu.VMEM((rows, pieces, capacity, lane), x.dtype),
            pltpu.VMEM((rows, half, capacity, lane), x.dtype),
            pltpu.VMEM((depth, slots), jnp.bfloat16),
            pltpu.VMEM((freqs, 8, depth), jnp.float32),
        ),
        in_specs=[pl.BlockSpec(memory_space=pl.ANY)] * 7,
        out_specs=[pl.BlockSpec(memory_space=pltpu.VMEM)] * 4,
        scratch_shapes=[
            pltpu.SMEM(counts.shape, counts.dtype),
            pltpu.SMEM(frequency.shape, frequency.dtype),
            pltpu.VMEM(val_band.shape, val_band.dtype),
            pltpu.VMEM(cond_band.shape, cond_band.dtype),
            pltpu.VMEM(val_energy.shape, val_energy.dtype),
            pltpu.VMEM(cond_energy.shape, cond_energy.dtype),
            dma((6,)),
            dma((pieces,)),
            dma((2, chips)),
            dma((2, chips, pieces)),
            dma((rows,)),
            dma((rows,)),
            dma((rows,)),
            dma((rows,)),
            dma((rows, half + 1)),
            pltpu.VMEM((half, capacity, lane), x.dtype),
            dma(()),
            dma((half,)),
            dma(()),
            dma(()),
            dma((half, 2)),
            dma(()),
            dma(()),
        ],
        compiler_params=pltpu.CompilerParams(
            collective_id=0, has_side_effects=True, vmem_limit_bytes=VMEM - room - SPARE
        ),
    )(x, counts, frequency, val_band, cond_band, val_energy, cond_energy)


def stream_kernel(weights, choose_ref, seg_ref, cols_ref, out_ref, turned, packed, buf, sem):
    freqs = weights.shape[0]
    rows, chunks, capacity, lane = seg_ref.shape
    slots, width = rows * capacity, packed.shape[1]
    firsts, parts = sem.shape[1], PARTS
    first, part = width // firsts, width // parts
    group = first // lane

    def put(chunk, f, n, wide):
        tall = pl.ds(pl.multiple_of(chunk * lane, lane), lane)
        across = pl.ds(n * wide, wide)
        return pltpu.make_async_copy(buf.at[f, :, across], out_ref.at[f, tall, across], sem.at[f, n])

    def turn(chunk):
        turned[...] = lax.dot_general(
            seg_ref[:, chunk].reshape(slots, lane), choose_ref[...], (((0,), (1,)), ((), ())),
            preferred_element_type=jnp.float32,
        )

    def scale(f):
        return (turned[...] * weights[f][:1]).astype(jnp.bfloat16)

    turn(0)
    for n in range(firsts):
        across = pl.ds(n * first, first)
        for p in range(n * group, (n + 1) * group):
            packed[:, p * lane : (p + 1) * lane] = jnp.dot(
                choose_ref[...], cols_ref[:, p].reshape(slots, lane), preferred_element_type=jnp.float32
            ).astype(jnp.bfloat16)
        for f in range(freqs):
            buf[f, :, across] = jnp.dot(scale(f), packed[:, across], preferred_element_type=jnp.float32)
            put(0, f, n, first).start()

    def body(t, carry):
        chunk, f = t // freqs, t % freqs

        @pl.when(f == 0)
        def _():
            turn(chunk)

        scaled = scale(f)
        for n in range(parts):
            @pl.when(chunk == 1)
            def _():
                for m in range(n * firsts // parts, (n + 1) * firsts // parts):
                    put(0, f, m, first).wait()

            @pl.when(chunk > 1)
            def _():
                put(chunk - 1, f, n, part).wait()

            across = pl.ds(n * part, part)
            buf[f, :, across] = jnp.dot(scaled, packed[:, across], preferred_element_type=jnp.float32)
            put(chunk, f, n, part).start()

        return carry

    lax.fori_loop(freqs, chunks * freqs, body, 0)

    def drain(f, carry):
        for n in range(parts):
            put(chunks - 1, f, n, part).wait()
        return carry

    lax.fori_loop(0, freqs, drain, 0)


def stream_product(weights, choose, seg, columns):
    freqs = weights.shape[0]
    rows, chunks, capacity, lane = seg.shape
    width, depth = columns.shape[1] * lane, choose.shape[0]
    vmem = pl.BlockSpec(memory_space=pltpu.VMEM)
    return pl.pallas_call(
        stream_kernel,
        out_shape=jax.ShapeDtypeStruct((freqs, chunks * lane, width), jnp.float32),
        in_specs=[vmem] * 4,
        out_specs=pl.BlockSpec(memory_space=pl.ANY),
        scratch_shapes=[
            pltpu.VMEM((lane, depth), jnp.float32),
            pltpu.VMEM((depth, width), jnp.bfloat16),
            pltpu.VMEM((freqs, lane, width), jnp.float32),
            pltpu.SemaphoreType.DMA((freqs, FIRST_PARTS)),
        ],
        compiler_params=pltpu.CompilerParams(vmem_limit_bytes=40 * 1024 * 1024),
    )(weights, choose, seg, columns)


def per_device(pair_elems, counts, val_band, cond_band, val_energy, cond_energy, frequency):
    rows, cols = lax.axis_size("row"), lax.axis_size("col")
    if cols == 4 and rows == 2 * cols and pair_elems.shape[1] % (128 * PIECES) == 0:
        columns, seg, choose, weights = plane_gather(
            pair_elems, counts, frequency, val_band, cond_band, val_energy, cond_energy, rows, cols
        )
        return stream_product(weights, choose, seg, columns)
    columns, seg, choose, weights = gather(
        pair_elems, counts, frequency, val_band, cond_band, val_energy, cond_energy, rows, cols
    )
    return product(weights, choose, seg, columns)


def solution(mesh):
    in_specs = (P("row", "col"), P(), P(), P(), P(), P(), P())
    out_specs = P(None, "row", "col")
    return jax.shard_map(
        per_device, mesh=mesh, in_specs=in_specs, out_specs=out_specs, check_vma=False
    )
```

```python
import functools
import math

import jax
import jax.numpy as jnp
from jax import lax
from jax.experimental import pallas as pl
from jax.experimental.pallas import tpu as pltpu
from jax.sharding import PartitionSpec as P

MESH = pl.DeviceIdType.MESH
LAG = 3
TILE = 1024
VMEM = 67043328
SPARE = 1024 * 1024
PIECES = 8
PARTS = 2
FIRST_PARTS = 4
ROLE_DELAYS = {True: {False: (3, 0), True: (6, 3)}, False: {False: (7, 7), True: (14, 14)}}
HOLD_STEP = 0
SPREAD_STEP = 10


def ring_place(c, count):
    if count == 4:
        return c + (c // 2) * (1 - 2 * (c % 2))
    return c


def gather_kernel(rows, cols, halves, x_ref, counts_hbm, freq_hbm, val_band_hbm, cond_band_hbm, val_energy_hbm,
                  cond_energy_hbm, cols_ref, seg_ref, choose_ref, weights_ref, counts_ref, freq_ref, val_band, cond_band,
                  val_energy, cond_energy, small_sem, own_sem, line_send, line_recv, mate_send, mate_recv, enter_send,
                  relay_send, ring_recv):
    r, c = lax.axis_index("row"), lax.axis_index("col")
    chips = rows // 2
    q, k = r // 2, r % 2
    pieces, lane = cols_ref.shape[1], cols_ref.shape[3]
    ratio = rows // cols
    chunks = ratio * halves
    place = ring_place(c, cols)
    source = r // ratio
    ring_next = [ring_place((place + 1) % cols, cols), ring_place((place + cols - 1) % cols, cols)]
    ahead = (place - ring_place(source, cols) + cols) % cols
    hops = [ahead, cols - ahead]
    up_ok, down_ok = q + 1 < chips, q >= 1

    own = [
        pltpu.make_async_copy(x_ref.at[:, pl.ds(p * lane, lane)], cols_ref.at[r, p], own_sem.at[p])
        for p in range(pieces)
    ]
    small = [
        pltpu.make_async_copy(src, dst, small_sem.at[i])
        for i, (src, dst) in enumerate((
            (counts_hbm, counts_ref), (freq_hbm, freq_ref), (val_band_hbm, val_band), (cond_band_hbm, cond_band),
            (val_energy_hbm, val_energy), (cond_energy_hbm, cond_energy),
        ))
    ]
    for copy in own + small:
        copy.start()
    barrier = pltpu.get_barrier_semaphore()

    def greet(row, col):
        pl.semaphore_signal(barrier, inc=1, device_id=(row, col), device_id_type=MESH)

    mate = 2 * q + 1 - k
    greet(mate, c)
    for nxt in ring_next:
        greet(2 * q, nxt)
        greet(2 * q + 1, nxt)

    @pl.when(up_ok)
    def _():
        greet(r + 2, c)

    @pl.when(down_ok)
    def _():
        greet(r - 2, c)

    pl.semaphore_wait(barrier, 5 + up_ok.astype(jnp.int32) + down_ok.astype(jnp.int32))
    for copy in own:
        copy.wait()

    def remote(src, dst, send, recv, row, col):
        return pltpu.make_async_remote_copy(
            src_ref=src, dst_ref=dst, send_sem=send, recv_sem=recv, device_id=(row, col), device_id_type=MESH
        )

    def block_of(stream, d, core):
        return 2 * (q - d if stream == 0 else q + d) + core

    def has(stream, d):
        return q >= d if stream == 0 else q + d < chips

    def line_copy(stream, d, j, b):
        ref = cols_ref.at[b, pl.ds(2 * j, 2)]
        row = r + 2 if stream == 0 else r - 2
        return remote(ref, ref, line_send.at[stream, d, j], line_recv.at[stream, d, j], row, c)

    def line_arrival(stream, d, j, b):
        ref = cols_ref.at[b, pl.ds(2 * j, 2)]
        return remote(ref, ref, line_send.at[stream, d, j], line_recv.at[stream, d - 1, j], mate, c)

    def mate_copy(b, j):
        ref = cols_ref.at[b, pl.ds(2 * j, 2)]
        return remote(ref, ref, mate_send.at[b, j], mate_recv.at[b, j], mate, c)

    def enter_copy(b, j, way):
        g = c * ratio + j // halves
        src = cols_ref.at[b, 2 * j + way]
        dst = seg_ref.at[b, 2 * (j % halves) + way]
        return remote(src, dst, enter_send.at[b, j, way], ring_recv.at[b, j % halves, way], g, ring_next[way])

    def relay_copy(b, j, way):
        ref = seg_ref.at[b, 2 * (j % halves) + way]
        return remote(ref, ref, relay_send.at[b, j % halves, way], ring_recv.at[b, j % halves, way], r, ring_next[way])

    def feeds(j):
        return (c * ratio + j // halves) // 2 == q

    def relays(j):
        return (source != c) & (j // halves == r % ratio)

    def onward(stream):
        return up_ok if stream == 0 else down_ok

    def line_part(step):
        d, j = step // chunks, step % chunks
        for stream in (0, 1):
            here = has(stream, d) if stream == 0 else has(stream, d) & (d > 0)
            b = block_of(stream, d, k)

            @pl.when(has(stream, d))
            def _():
                @pl.when(d > 0)
                def _():
                    line_arrival(stream, d, j, b).wait_recv()

                @pl.when(onward(stream))
                def _():
                    line_copy(stream, d, j, b).start()

            @pl.when(here)
            def _():
                mate_copy(b, j).start()

                @pl.when(feeds(j))
                def _():
                    for way in (0, 1):
                        enter_copy(b, j, way).start()

    def ring_part(step, way):
        d, j = step // chunks, step % chunks

        @pl.when(relays(j))
        def _():
            for stream in (0, 1):
                here = has(stream, d) if stream == 0 else has(stream, d) & (d > 0)

                @pl.when(here)
                def _():
                    for core in (0, 1):
                        b = block_of(stream, d, core)
                        relay_copy(b, j, way).wait_recv()

                        @pl.when(ring_next[way] != source)
                        def _():
                            relay_copy(b, j, way).start()

    steps = chunks * chips

    def body(step, carry):
        @pl.when(step < steps)
        def _():
            line_part(step)

        for way in (0, 1):
            late = step - LAG * hops[way]

            @pl.when((late >= 0) & (late < steps))
            def _():
                ring_part(late, way)

        return carry

    lax.fori_loop(0, chunks, body, 0)
    for copy in small:
        copy.wait()
    capacity, (depth, slots) = x_ref.shape[0], choose_ref.shape
    place_of = slot_target(counts_ref, (1, slots), 1, capacity)
    choose = (lax.broadcasted_iota(jnp.int32, (depth, slots), 0) == place_of).astype(jnp.float32)
    gap = pick(cond_band, cond_energy) - pick(val_band, val_energy)
    gap = lax.dot_general(
        gap, choose, (((1,), (1,)), ((), ())), precision=lax.Precision.HIGHEST, preferred_element_type=jnp.float32
    )
    for f in range(weights_ref.shape[0]):
        weights_ref[f] = -4.0 * gap / (gap * gap + freq_ref[f] * freq_ref[f])
    choose_ref[...] = choose.astype(jnp.bfloat16)
    lax.fori_loop(chunks, steps + LAG * (cols - 1), body, 0)

    def finish(step, carry):
        d, j = step // chunks, step % chunks
        for stream in (0, 1):
            here = has(stream, d) if stream == 0 else has(stream, d) & (d > 0)
            b = block_of(stream, d, k)
            theirs = block_of(stream, d, 1 - k)

            @pl.when(has(stream, d) & onward(stream))
            def _():
                line_copy(stream, d, j, b).wait_send()

            @pl.when(here)
            def _():
                mate_copy(b, j).wait_send()
                mate_copy(theirs, j).wait_recv()

                @pl.when(feeds(j))
                def _():
                    for way in (0, 1):
                        enter_copy(b, j, way).wait_send()

                @pl.when(relays(j))
                def _():
                    for core in (0, 1):
                        e = block_of(stream, d, core)
                        for way in (0, 1):
                            @pl.when(ring_next[way] != source)
                            def _():
                                relay_copy(e, j, way).wait_send()

        return carry

    lax.fori_loop(0, steps, finish, 0)

    @pl.when(source == c)
    def _():
        here = pltpu.make_async_copy(cols_ref.at[:, pl.ds((r % ratio) * 2 * halves, 2 * halves)], seg_ref, own_sem.at[0])
        here.start()
        here.wait()


def gather(x, counts, frequency, val_band, cond_band, val_energy, cond_energy, rows, cols):
    capacity, width = x.shape
    slots = rows * capacity
    live = slots * 5 // 8
    depth = pl.cdiv(live, 256) * 256
    ratio = rows // cols
    seg_width = width // ratio
    halves = 2 if seg_width % 512 == 0 else 1
    chunks, chips = ratio * halves, rows // 2
    dma = pltpu.SemaphoreType.DMA
    room = 2 * (slots * (width + seg_width) + depth * slots) + 4 * 8 * depth * frequency.shape[0]
    return pl.pallas_call(
        functools.partial(gather_kernel, rows, cols, halves),
        out_shape=(
            pltpu.VMEM((rows, 2 * chunks, capacity, seg_width // halves // 2), x.dtype),
            pltpu.VMEM((rows, 2 * halves, capacity, seg_width // halves // 2), x.dtype),
            pltpu.VMEM((depth, slots), jnp.bfloat16),
            pltpu.VMEM((frequency.shape[0], 8, depth), jnp.float32),
        ),
        in_specs=[pl.BlockSpec(memory_space=pl.ANY)] * 7,
        out_specs=[pl.BlockSpec(memory_space=pltpu.VMEM)] * 4,
        scratch_shapes=[
            pltpu.SMEM(counts.shape, counts.dtype),
            pltpu.SMEM(frequency.shape, frequency.dtype),
            pltpu.VMEM(val_band.shape, val_band.dtype),
            pltpu.VMEM(cond_band.shape, cond_band.dtype),
            pltpu.VMEM(val_energy.shape, val_energy.dtype),
            pltpu.VMEM(cond_energy.shape, cond_energy.dtype),
            dma((6,)),
            dma((2 * chunks,)),
            dma((2, chips, chunks)),
            dma((2, chips, chunks)),
            dma((rows, chunks)),
            dma((rows, chunks)),
            dma((rows, chunks, 2)),
            dma((rows, halves, 2)),
            dma((rows, halves, 2)),
        ],
        compiler_params=pltpu.CompilerParams(
            collective_id=0, has_side_effects=True, vmem_limit_bytes=VMEM - room - SPARE
        ),
    )(x, counts, frequency, val_band, cond_band, val_energy, cond_energy)


def exact_dot(a, b):
    return lax.dot_general(
        a, b, (((1,), (0,)), ((), ())), precision=lax.Precision.HIGHEST, preferred_element_type=jnp.float32
    )


def pick(band_ref, table_ref):
    levels, slots = table_ref.shape[0], band_ref.shape[0]
    hit = lax.broadcasted_iota(jnp.int32, (levels, slots), 0) == band_ref[...][None, :]
    return exact_dot(jnp.broadcast_to(table_ref[...][None, :], (8, levels)), hit.astype(jnp.float32))


def slot_target(counts_ref, shape, axis, capacity):
    slot = lax.broadcasted_iota(jnp.int32, shape, axis)
    target = jnp.full(shape, -1, jnp.int32)
    before = 0
    for block in range(counts_ref.shape[0]):
        inside = slot - block * capacity
        live = (inside >= 0) & (inside < counts_ref[block])
        target = jnp.where(live, inside + before, target)
        before = before + counts_ref[block]
    return target


def product_kernel(weights, choose_ref, seg_ref, cols_ref, out_ref, packed, turned, scaled):
    which, n = pl.program_id(0), pl.program_id(1)
    tile = out_ref.shape[2]
    rows, pieces, capacity, lane = cols_ref.shape
    slots = rows * capacity

    @pl.when((n == 0) & (which == 0))
    def _():
        choose = choose_ref[...]
        for p in range(pieces):
            piece = cols_ref[:, p].reshape(slots, lane)
            packed[:, p * lane : (p + 1) * lane] = jnp.dot(
                choose, piece, preferred_element_type=jnp.float32
            ).astype(jnp.bfloat16)
        for p in range(seg_ref.shape[1]):
            piece = seg_ref[:, p].reshape(slots, lane)
            turned[p * lane : (p + 1) * lane, :] = lax.dot_general(
                piece, choose, (((0,), (1,)), ((), ())), preferred_element_type=jnp.float32
            ).astype(jnp.bfloat16)

    @pl.when(n == 0)
    def _():
        scaled[...] = (turned[...].astype(jnp.float32) * weights[which][:1]).astype(jnp.bfloat16)

    start = pl.multiple_of(n * tile, tile)
    out_ref[0] = jnp.dot(scaled[...], packed[:, pl.ds(start, tile)], preferred_element_type=jnp.float32)


def product(weights, choose, seg, columns):
    freqs = weights.shape[0]
    rows, pieces, capacity, lane = columns.shape
    width, seg_width = pieces * lane, seg.shape[1] * lane
    depth = choose.shape[0]
    tile = math.gcd(width, TILE)
    vmem = pl.BlockSpec(memory_space=pltpu.VMEM)
    return pl.pallas_call(
        product_kernel,
        out_shape=jax.ShapeDtypeStruct((freqs, seg_width, width), jnp.float32),
        grid=(freqs, width // tile),
        in_specs=[vmem] * 4,
        out_specs=pl.BlockSpec((1, seg_width, tile), lambda f, n: (f, 0, n)),
        scratch_shapes=[
            pltpu.VMEM((depth, width), jnp.bfloat16),
            pltpu.VMEM((seg_width, depth), jnp.bfloat16),
            pltpu.VMEM((seg_width, depth), jnp.bfloat16),
        ],
        compiler_params=pltpu.CompilerParams(vmem_limit_bytes=40 * 1024 * 1024),
    )(weights, choose, seg, columns)


def plane_gather_kernel(rows, cols, x_ref, counts_hbm, freq_hbm, val_band_hbm, cond_band_hbm, val_energy_hbm,
                        cond_energy_hbm, cols_ref, seg_ref, choose_ref, weights_ref, counts_ref, freq_ref,
                        val_band, cond_band, val_energy, cond_energy, small_sem, own_sem, line_send, line_recv, mate_send,
                        mate_recv, enter_send, relay_send, seg_recv, held, held_send, held_recv, direct_send, aid_send,
                        aid_recv, aid_mate_send, aid_mate_recv):
    r, c = lax.axis_index("row"), lax.axis_index("col")
    chips = rows // 2
    q, k = r // 2, r % 2
    pieces, lane = cols_ref.shape[1], cols_ref.shape[3]
    half = pieces // 2
    place = ring_place(c, cols)
    rel = (place - ring_place(q, cols) + cols) % cols

    def chip_at(position):
        return ring_place((position + cols) % cols, cols)

    near = [chip_at(place + 1), chip_at(place - 1)]
    is_source = rel == 0
    up_ok, down_ok = q + 1 < chips, q >= 1
    end = ~(up_ok & down_ok)
    target = jnp.where(q == 1, 0, chips - 1)
    target_rel = (place - ring_place(target, cols) + cols) % cols
    helper = ((q == 1) | (q == chips - 2)) & ~end
    beside = jnp.where(q == 0, 1, chips - 2)
    aids = [(h * half + half // 2, cols - 1) for h in (0, 1)] + [(h * half + half // 2 + 1, 2) for h in (0, 1)]

    own = [
        pltpu.make_async_copy(x_ref.at[:, pl.ds(p * lane, lane)], cols_ref.at[r, p], own_sem.at[p])
        for p in range(pieces)
    ]
    small = [
        pltpu.make_async_copy(src, dst, small_sem.at[i])
        for i, (src, dst) in enumerate((
            (counts_hbm, counts_ref), (freq_hbm, freq_ref), (val_band_hbm, val_band), (cond_band_hbm, cond_band),
            (val_energy_hbm, val_energy), (cond_energy_hbm, cond_energy),
        ))
    ]
    for copy in own + small:
        copy.start()
    barrier = pltpu.get_barrier_semaphore()

    def greet(row, col):
        pl.semaphore_signal(barrier, inc=1, device_id=(row, col), device_id_type=MESH)

    mate = 2 * q + 1 - k
    across = end | (target_rel % 2 == 0) | (rel % 2 == 0)

    @pl.when(across)
    def _():
        greet(r, chip_at(place + 2))

    crossing = (end & (rel >= 2)) | (helper & (target_rel >= 2))

    @pl.when(crossing)
    def _():
        greet(2 * jnp.where(end, beside, target) + 1 - k, c)

    @pl.when(up_ok)
    def _():
        greet(r + 2, c)

    @pl.when(down_ok)
    def _():
        greet(r - 2, c)

    @pl.when(is_source)
    def _():
        greet(mate, near[0])
        greet(mate, near[1])
        greet(mate, chip_at(place + 2))

    @pl.when(~is_source)
    def _():
        greet(mate, chip_at(place - rel))

    greet(r, near[0])
    greet(r, near[1])
    greet(mate, c)
    calls = 3 + jnp.where(is_source, 3, 1) + up_ok.astype(jnp.int32) + down_ok.astype(jnp.int32)
    pl.semaphore_wait(barrier, calls + across.astype(jnp.int32) + crossing.astype(jnp.int32))
    for copy in own:
        copy.wait()

    def remote(src, dst, send, recv, row, col):
        return pltpu.make_async_remote_copy(
            src_ref=src, dst_ref=dst, send_sem=send, recv_sem=recv, device_id=(row, col), device_id_type=MESH
        )

    def block_of(stream, d, core):
        return 2 * (q - d if stream == 0 else q + d) + core

    def has(stream, d):
        return q >= d if stream == 0 else q + d < chips

    def here(stream, d):
        return has(stream, d) if stream == 0 else has(stream, d) & (d > 0)

    def onward(stream):
        return up_ok if stream == 0 else down_ok

    def line_copy(stream, d, piece, arrival):
        row = r + 2 if stream == 0 else r - 2
        return remote(piece, piece, line_send.at[stream, d], arrival, row, c)

    def mate_copy(b, piece):
        return remote(piece, piece, mate_send.at[b], mate_recv.at[b], mate, c)

    def enter_copy(b, p, way):
        arrival = seg_recv.at[b, jnp.where(p % 2 == way, p % half, half)]
        return remote(cols_ref.at[b, p], seg_ref.at[b, p % half], enter_send.at[b], arrival, 2 * q + p // half, near[way])

    def direct_copy(b, p):
        arrival = seg_recv.at[b, half]
        return remote(cols_ref.at[b, p], seg_ref.at[b, p % half], direct_send, arrival, 2 * q + p // half, chip_at(place + 2))

    def relay_copy(d, b, p, way):
        last = (rel == 2) | tree(d)
        piece = seg_ref.at[b, p % half]
        return remote(piece, piece, relay_send.at[b], seg_recv.at[b, jnp.where(last, half, p % half)], r, near[way])

    def await_sends(ref, sem):
        remote(ref, ref, sem, mate_recv.at[0], mate, c).wait_send()

    def await_arrivals(ref, sem):
        remote(ref, ref, mate_send.at[0], sem, mate, c).wait_recv()

    def tree(d):
        return d == jnp.maximum(q, chips - 1 - q)

    def aided(d, p):
        return end & (d == 1) & (p % half >= half // 2)

    def enters(d, p, way):
        return (p % 2 == way) | tree(d)

    def forwards(d, p, way):
        carries = (rel == (1 if way == 0 else cols - 1)) | ((rel == 2) & ~tree(d))
        return (p % 2 == way) & carries & ~aided(d, p)

    def held_copy(i, p, line):
        dst = held.at[i]
        return remote(cols_ref.at[r, p], dst, held_send, held_recv.at[i], r, chip_at(place + line))

    def aid_line_copy(i, p):
        b = r
        dst = seg_ref.at[b, p % half]
        return remote(held.at[i], dst, held_send, seg_recv.at[b, p % half], 2 * target + p // half, c)

    def aid_copy(b, p, turn):
        piece = seg_ref.at[b, p % half]
        return remote(piece, piece, aid_send, seg_recv.at[b, p % half], r, chip_at(place + turn))

    def aid_home_copy(i, core, b, p, line):
        return remote(seg_ref.at[b, p % half], cols_ref.at[b, p], aid_send, aid_recv.at[i, core], r, chip_at(place - line))

    def aid_mate_copy(b, p):
        piece = cols_ref.at[b, p]
        return remote(piece, piece, aid_mate_send, aid_mate_recv, mate, c)

    def feed(d, p, b):
        @pl.when(is_source)
        def _():
            for way in (0, 1):
                @pl.when(enters(d, p, way))
                def _():
                    enter_copy(b, p, way).start()

    def begin(p, carry):
        for stream in (0, 1):
            toward = target > q if stream == 0 else target < q
            spared = helper & (target_rel == 0) & toward & (p % half >= half // 2)

            paired = helper & (target_rel != 0) & toward

            @pl.when(onward(stream) & ~spared & ~paired)
            def _():
                line_copy(stream, 0, cols_ref.at[r, p], line_recv.at[stream, 0, p]).start()

            @pl.when(onward(stream) & paired & (p % 2 == 1))
            def _():
                line_copy(stream, 0, cols_ref.at[r, pl.ds(p - 1, 2)], line_recv.at[stream, 0, p]).start()

        feed(0, p, r)
        mate_copy(r, cols_ref.at[r, p]).start()
        return carry

    @pl.when(helper & (target_rel == 0))
    def _():
        for i, (p, line) in enumerate(aids):
            held_copy(i, p, line).start()

    lax.fori_loop(0, pieces, begin, 0)

    for copy in small:
        copy.wait()
    capacity, (depth, slots) = x_ref.shape[0], choose_ref.shape
    place_of = slot_target(counts_ref, (1, slots), 1, capacity)
    choose = (lax.broadcasted_iota(jnp.int32, (depth, slots), 0) == place_of).astype(jnp.float32)
    gap = pick(cond_band, cond_energy) - pick(val_band, val_energy)
    gap = lax.dot_general(
        gap, choose, (((1,), (1,)), ((), ())), precision=lax.Precision.HIGHEST, preferred_element_type=jnp.float32
    )
    for f in range(weights_ref.shape[0]):
        weights_ref[f] = -4.0 * gap / (gap * gap + freq_ref[f] * freq_ref[f])
    choose_ref[...] = choose.astype(jnp.bfloat16)

    def hold_part():
        for i, (p, line) in enumerate(aids):
            @pl.when(helper & (target_rel == line))
            def _():
                await_arrivals(held.at[i], held_recv.at[i])
                aid_line_copy(i, p).start()

    def spread_part():
        for i, (p, line) in enumerate(aids):
            @pl.when(end & (rel == line) & (k == p // half))
            def _():
                for core in (0, 1):
                    b = 2 * beside + core
                    await_arrivals(seg_ref.at[b, p % half], seg_recv.at[b, p % half])
                    aid_home_copy(i, core, b, p, line).start()
                    for turn in range(1, cols):
                        if (line + turn) % cols != 0:
                            aid_copy(b, p, turn).start()

    def land_part():
        for i, (p, line) in enumerate(aids):
            @pl.when(end & is_source & (k == p // half))
            def _():
                for core in (0, 1):
                    b = 2 * beside + core
                    await_arrivals(cols_ref.at[b, p], aid_recv.at[i, core])
                    aid_mate_copy(b, p).start()

    def line_step(d, p, ends, source):
        if ends:
            flow = jnp.where(q == 0, 1, 0)
            streams = [(flow, 2 * (q + jnp.where(q == 0, d, -d)) + k, None, (d > 0) & (d < chips))]
        else:
            streams = [
                (0, 2 * (q - d) + k, r + 2, (d > 0) & (d <= q)),
                (1, 2 * (q + d) + k, r - 2, (d > 0) & (d < chips - q)),
            ]
        paired = ends and not source
        if paired and p % 2 == 0:
            return
        for stream, b, row, present in streams:
            if ends and source and p % half >= half // 2:
                present = present & (d > 1)

            @pl.when(present)
            def _():
                piece = cols_ref.at[b, pl.ds(p - 1, 2)] if paired else cols_ref.at[b, p]
                await_arrivals(piece, line_recv.at[stream, d - 1, p])
                if row is not None:
                    double = (target_rel != 0) & ((target > q) if stream == 0 else (target < q))

                    @pl.when(~double)
                    def _():
                        line_copy(stream, d, piece, line_recv.at[stream, d, p]).start()

                    if p % 2 == 1:
                        @pl.when(double)
                        def _():
                            line_copy(stream, d, cols_ref.at[b, pl.ds(p - 1, 2)], line_recv.at[stream, d, p]).start()

                if source:
                    @pl.when(tree(d))
                    def _():
                        if p == pieces - 1:
                            direct_copy(b, p).start()
                        enter_copy(b, p, 1 - p % 2).start()

                    enter_copy(b, p, p % 2).start()

                mate_copy(b, piece).start()

    def relay_step(d, p, ends, opposite, least, most):
        mine = k == p // half
        if ends:
            blocks = [(2 * (q + jnp.where(q == 0, d, -d)), (d >= least) & (d <= most))]
            if p % half >= half // 2:
                mine = mine & (d != 1)
        else:
            blocks = [(2 * (q - d), (d >= least) & (d <= most) & (d <= q)), (2 * (q + d), (d >= least) & (d <= most) & (d > 0) & (d < chips - q))]
        if opposite:
            mine = mine & ~tree(d)
        else:
            mine = mine & (rel == (1 if p % 2 == 0 else cols - 1))

        @pl.when(mine)
        def _():
            for first, present in blocks:
                @pl.when(present)
                def _():
                    for core in (0, 1):
                        b = first + core
                        await_arrivals(seg_ref.at[b, p % half], seg_recv.at[b, p % half])

                        @pl.when(~tree(d) | (p < pieces - 1))
                        def _():
                            relay_copy(d, b, p, p % 2).start()

    def role(ends, place_in_ring):
        source, opposite = place_in_ring == 0, place_in_ring == 2
        near_delay, far_delay = ROLE_DELAYS[ends][opposite]

        def body(d, carry):
            for p in range(pieces):
                line_step(d, p, ends, source)
                step = d - 1
                if not ends and p == HOLD_STEP % pieces:
                    @pl.when(step == HOLD_STEP // pieces)
                    def _():
                        hold_part()

                if ends and not source and p == SPREAD_STEP % pieces:
                    @pl.when(step == SPREAD_STEP // pieces)
                    def _():
                        spread_part()

                if not source:
                    for delay, least, most in ((near_delay, 0, 1), (far_delay, 2, chips - 1)):
                        shift, late = divmod(p - delay, pieces)
                        relay_step(d + shift, late, ends, opposite, least, most)

            return carry

        turns = 0 if source else max(0, -(-max(near_delay, far_delay) // pieces))
        start = 1 if source else 0
        lax.fori_loop(start, chips + turns, body, 0)

    for ends in (False, True):
        for kind in (0, 1, 2):
            here_now = (rel == kind) if kind != 1 else (rel % 2 == 1)

            @pl.when(here_now & (end if ends else ~end))
            def _():
                role(ends, kind)

    @pl.when(end & is_source)
    def _():
        land_part()

    def gather_end(d, carry):
        for stream in (0, 1):
            @pl.when(here(stream, d))
            def _():
                b = block_of(stream, d, 1 - k)
                partial = is_source & aided(d, pieces - 1)

                @pl.when(partial)
                def _():
                    await_arrivals(cols_ref.at[b, pl.ds(0, half)], mate_recv.at[b])

                @pl.when(~partial)
                def _():
                    await_arrivals(cols_ref.at[b], mate_recv.at[b])

        return carry

    lax.fori_loop(0, chips, gather_end, 0)

    @pl.when(end & is_source)
    def _():
        await_arrivals(cols_ref.at[0, pl.ds(0, half)], aid_mate_recv)

    stay = pltpu.make_async_copy(cols_ref.at[:, pl.ds(k * half, half)], seg_ref, own_sem.at[0])

    @pl.when(is_source)
    def _():
        stay.start()

    def finish(d, carry):
        part = aided(d, pieces - 1)
        for stream in (0, 1):
            b = block_of(stream, d, k)
            toward = target > q if stream == 0 else target < q
            spared = helper & (target_rel == 0) & toward & (d == 0)

            @pl.when(has(stream, d) & onward(stream) & spared)
            def _():
                await_sends(cols_ref.at[b, pl.ds(0, half)], line_send.at[stream, d])

            @pl.when(has(stream, d) & onward(stream) & ~spared)
            def _():
                await_sends(cols_ref.at[b], line_send.at[stream, d])

            @pl.when(here(stream, d))
            def _():
                @pl.when(is_source & part)
                def _():
                    await_sends(cols_ref.at[b, pl.ds(0, half)], mate_send.at[b])
                    await_sends(cols_ref.at[b, pl.ds(0, half)], enter_send.at[b])

                @pl.when(~(is_source & part))
                def _():
                    await_sends(cols_ref.at[b], mate_send.at[b])

                @pl.when(is_source & tree(d))
                def _():
                    await_sends(cols_ref.at[pl.ds(0, 2)], enter_send.at[b])
                    await_sends(cols_ref.at[b, 0], direct_send)

                @pl.when(is_source & ~tree(d) & ~part)
                def _():
                    await_sends(cols_ref.at[b], enter_send.at[b])

                for core in (0, 1):
                    e = block_of(stream, d, core)
                    for some, count in ((part, half // 2), (~part, half)):
                        @pl.when(some & ((rel == 1) | (rel == cols - 1)))
                        def _():
                            fewer = (rel == cols - 1) & tree(d) & (k == 1)

                            @pl.when(fewer)
                            def _():
                                await_sends(seg_ref.at[e, pl.ds(0, max(count // 2 - 1, 1))], relay_send.at[e])

                            @pl.when(~fewer)
                            def _():
                                await_sends(seg_ref.at[e, pl.ds(0, count // 2)], relay_send.at[e])

                            await_arrivals(seg_ref.at[e, pl.ds(0, count // 2)], seg_recv.at[e, half])

                        @pl.when(some & (rel == 2) & ~tree(d))
                        def _():
                            await_sends(seg_ref.at[e, pl.ds(0, count)], relay_send.at[e])

                    @pl.when((rel == 2) & tree(d))
                    def _():
                        await_arrivals(seg_ref.at[e], seg_recv.at[e, half])

        return carry

    for i, (p, line) in enumerate(aids):
        @pl.when(end & ~is_source & (rel != line) & (k == p // half))
        def _():
            for core in (0, 1):
                b = 2 * beside + core
                await_arrivals(seg_ref.at[b, p % half], seg_recv.at[b, p % half])

    for line in range(1, cols):
        for core in (0, 1):
            count = sum(1 for p, other in aids if other == line and p // half == core)
            if count > 0:
                @pl.when(end & (rel == line) & (k == core))
                def _():
                    await_sends(cols_ref.at[pl.ds(0, cols - 1), pl.ds(0, 2 * count)], aid_send)

    for line in range(1, cols):
        count = sum(1 for _, other in aids if other == line)
        if count > 0:
            @pl.when(helper & (target_rel == line))
            def _():
                await_sends(held.at[pl.ds(0, count)], held_send)

    @pl.when(helper & (target_rel == 0))
    def _():
        await_sends(held, held_send)

    @pl.when(end & is_source)
    def _():
        await_sends(cols_ref.at[0, pl.ds(0, half)], aid_mate_send)

    lax.fori_loop(0, chips, finish, 0)

    @pl.when(is_source)
    def _():
        stay.wait()


def plane_gather(x, counts, frequency, val_band, cond_band, val_energy, cond_energy, rows, cols):
    capacity, width = x.shape
    slots = rows * capacity
    depth = pl.cdiv(slots * 5 // 8, 256) * 256
    chips, pieces = rows // 2, PIECES
    half, lane, freqs = pieces // 2, width // pieces, frequency.shape[0]
    dma = pltpu.SemaphoreType.DMA
    room = 2 * (slots * width * 3 // 2 + depth * slots) + 4 * 8 * depth * freqs
    return pl.pallas_call(
        functools.partial(plane_gather_kernel, rows, cols),
        out_shape=(
            pltpu.VMEM((rows, pieces, capacity, lane), x.dtype),
            pltpu.VMEM((rows, half, capacity, lane), x.dtype),
            pltpu.VMEM((depth, slots), jnp.bfloat16),
            pltpu.VMEM((freqs, 8, depth), jnp.float32),
        ),
        in_specs=[pl.BlockSpec(memory_space=pl.ANY)] * 7,
        out_specs=[pl.BlockSpec(memory_space=pltpu.VMEM)] * 4,
        scratch_shapes=[
            pltpu.SMEM(counts.shape, counts.dtype),
            pltpu.SMEM(frequency.shape, frequency.dtype),
            pltpu.VMEM(val_band.shape, val_band.dtype),
            pltpu.VMEM(cond_band.shape, cond_band.dtype),
            pltpu.VMEM(val_energy.shape, val_energy.dtype),
            pltpu.VMEM(cond_energy.shape, cond_energy.dtype),
            dma((6,)),
            dma((pieces,)),
            dma((2, chips)),
            dma((2, chips, pieces)),
            dma((rows,)),
            dma((rows,)),
            dma((rows,)),
            dma((rows,)),
            dma((rows, half + 1)),
            pltpu.VMEM((half, capacity, lane), x.dtype),
            dma(()),
            dma((half,)),
            dma(()),
            dma(()),
            dma((half, 2)),
            dma(()),
            dma(()),
        ],
        compiler_params=pltpu.CompilerParams(
            collective_id=0, has_side_effects=True, vmem_limit_bytes=VMEM - room - SPARE
        ),
    )(x, counts, frequency, val_band, cond_band, val_energy, cond_energy)


def stream_kernel(weights, choose_ref, seg_ref, cols_ref, out_ref, turned, ready, packed, buf, sem):
    freqs = weights.shape[0]
    rows, chunks, capacity, lane = seg_ref.shape
    slots, width = rows * capacity, packed.shape[1]
    firsts, parts = sem.shape[1], PARTS
    first, part = width // firsts, width // parts
    group = first // lane

    def put(chunk, f, n, wide):
        tall = pl.ds(pl.multiple_of(chunk * lane, lane), lane)
        across = pl.ds(n * wide, wide)
        return pltpu.make_async_copy(buf.at[f, :, across], out_ref.at[f, tall, across], sem.at[f, n])

    def turn(chunk):
        turned[...] = lax.dot_general(
            seg_ref[:, chunk].reshape(slots, lane), choose_ref[...], (((0,), (1,)), ((), ())),
            preferred_element_type=jnp.float32,
        )

    def scale(f):
        return (turned[...] * weights[f][:1]).astype(jnp.bfloat16)

    turn(0)
    for n in range(firsts):
        across = pl.ds(n * first, first)
        for p in range(n * group, (n + 1) * group):
            packed[:, p * lane : (p + 1) * lane] = jnp.dot(
                choose_ref[...], cols_ref[:, p].reshape(slots, lane), preferred_element_type=jnp.float32
            ).astype(jnp.bfloat16)
        for f in range(freqs):
            if n == 0:
                ready[f] = scale(f)
            buf[f, :, across] = jnp.dot(ready[f], packed[:, across], preferred_element_type=jnp.float32)
            put(0, f, n, first).start()

    def body(t, carry):
        chunk, f = t // freqs, t % freqs

        @pl.when(f == 0)
        def _():
            turn(chunk)

        scaled = scale(f)
        for n in range(parts):
            @pl.when(chunk == 1)
            def _():
                for m in range(n * firsts // parts, (n + 1) * firsts // parts):
                    put(0, f, m, first).wait()

            @pl.when(chunk > 1)
            def _():
                put(chunk - 1, f, n, part).wait()

            across = pl.ds(n * part, part)
            buf[f, :, across] = jnp.dot(scaled, packed[:, across], preferred_element_type=jnp.float32)
            put(chunk, f, n, part).start()

        return carry

    lax.fori_loop(freqs, chunks * freqs, body, 0)

    def drain(f, carry):
        for n in range(parts):
            put(chunks - 1, f, n, part).wait()
        return carry

    lax.fori_loop(0, freqs, drain, 0)


def stream_product(weights, choose, seg, columns):
    freqs = weights.shape[0]
    rows, chunks, capacity, lane = seg.shape
    width, depth = columns.shape[1] * lane, choose.shape[0]
    vmem = pl.BlockSpec(memory_space=pltpu.VMEM)
    return pl.pallas_call(
        stream_kernel,
        out_shape=jax.ShapeDtypeStruct((freqs, chunks * lane, width), jnp.float32),
        in_specs=[vmem] * 4,
        out_specs=pl.BlockSpec(memory_space=pl.ANY),
        scratch_shapes=[
            pltpu.VMEM((lane, depth), jnp.float32),
            pltpu.VMEM((freqs, lane, depth), jnp.bfloat16),
            pltpu.VMEM((depth, width), jnp.bfloat16),
            pltpu.VMEM((freqs, lane, width), jnp.float32),
            pltpu.SemaphoreType.DMA((freqs, FIRST_PARTS)),
        ],
        compiler_params=pltpu.CompilerParams(vmem_limit_bytes=40 * 1024 * 1024),
    )(weights, choose, seg, columns)


def per_device(pair_elems, counts, val_band, cond_band, val_energy, cond_energy, frequency):
    rows, cols = lax.axis_size("row"), lax.axis_size("col")
    if cols == 4 and rows == 2 * cols and pair_elems.shape[1] % (128 * PIECES) == 0:
        columns, seg, choose, weights = plane_gather(
            pair_elems, counts, frequency, val_band, cond_band, val_energy, cond_energy, rows, cols
        )
        return stream_product(weights, choose, seg, columns)
    columns, seg, choose, weights = gather(
        pair_elems, counts, frequency, val_band, cond_band, val_energy, cond_energy, rows, cols
    )
    return product(weights, choose, seg, columns)


def solution(mesh):
    in_specs = (P("row", "col"), P(), P(), P(), P(), P(), P())
    out_specs = P(None, "row", "col")
    return jax.shard_map(
        per_device, mesh=mesh, in_specs=in_specs, out_specs=out_specs, check_vma=False
    )
```
